128 devices in a mesh: replica: 2 (over core), shard: 64 (over z, y, x).
Axes of the slice: x: 4, y: 4, z: 4, core: 2. Of those that a mesh axis runs over, the one named last changes fastest.
Arguments:
- dense_input: bfloat16 [16384, 256], P(('replica', 'shard')), may hold values from -6 to 6
- bag_rows: int32 [16384, 2, 16], P(('replica', 'shard')), may hold values from 0 to 32767, as said below
- bag_lengths: int32 [16384, 2], P(('replica', 'shard')), may hold values from 1 to 16
- bag_weights: bfloat16 [16384, 2, 16], P(('replica', 'shard')), may hold values from 0.5 to 2
- labels: int32 [16384], P(('replica', 'shard')), may hold values 0 or 1
- embedding: float32 [32768, 2, 256], P('shard'), may hold values from -2 to 2
- first_moment: float32 [32768, 2, 256], P('shard'), may hold values from -6 to 6
- second_moment: float32 [32768, 2], P('shard'), may hold values from 0.5 to 8
- cross_weight: bfloat16 [768, 768], replicated, may hold values from -0.21875 to 0.21875
- hidden_weight: bfloat16 [768, 4096], replicated, may hold values from -0.21875 to 0.21875
- head_weight: bfloat16 [4096], replicated, may hold values from -0.09375 to 0.09375
Outputs:
- new_first: float32 [32768, 2, 256], P('shard')
- new_second: float32 [32768, 2], P('shard')
- row_step: float32 [32768, 2, 256], P('shard')
The draws below stay inside these ranges and needn't reach their ends.
Inputs may be any that keep to these rules, and one draw needn't show every extreme that they name: `bag_rows`: call the rows k * 512 to (k + 1) * 512 - 1 those of owner k. For each table, all slots of one device's 128 samples (used or not) name at most 32 distinct rows of any one owner, and every device names exactly 32 distinct rows of some owner in each table. Row indices may be held and sent in any lossless form.
All inputs are finite; a program needn't handle non-finite values. No bound on the sum of `labels` on one device may be relied on, other than what follows from the above.
Results may differ from the reference program's by a relative error of at most 0.0038.
The reference program's roundings to bfloat16 on the way count: a program that leaves them out, or rounds other values in their place, can miss the bound.
Values may be sent and summed in bfloat16 or wider, within the bound.
No kernel may reach another device: no remote copies, remote signals or barrier semaphores. Data moves between devices by JAX's collectives and lax.ppermute only.
A program may use at most 128 MiB of HBM per device.

```python
import math
import jax
import jax.numpy as jnp
from jax import lax

E = 256
HID = 4096
NT = 2
MAXBAG = 16
CAP = 32
B_DEV = 128
ROWS_DEV = 512
D0 = 768
ROWS = 32768
BATCH = 16384
N_REPLICA = 2
N_SHARD = 64


def draw_bag_rows(key, part):
    groups = BATCH // B_DEV
    owners = ROWS // ROWS_DEV
    keys = jax.random.split(jax.random.fold_in(key, 7301), 6)
    perm_keys = jax.random.split(keys[0], groups * NT * owners)
    picks = jax.vmap(lambda one: jax.random.permutation(one, ROWS_DEV)[:CAP])(perm_keys).reshape(groups, NT, owners, CAP)
    order_keys = jax.random.split(keys[1], groups * NT)
    owner_order = jax.vmap(lambda one: jax.random.permutation(one, owners))(order_keys).reshape(groups, NT, owners)
    shape = (groups, B_DEV, NT, MAXBAG)
    owner_rank = jnp.minimum(jax.random.randint(keys[2], shape, 0, owners), jax.random.randint(keys[3], shape, 0, owners))
    choose = jnp.minimum(jax.random.randint(keys[4], shape, 0, CAP), jax.random.randint(keys[5], shape, 0, CAP))
    sample_ids = jnp.arange(B_DEV, dtype=jnp.int32)[None, :, None]
    forced = sample_ids < CAP
    owner_rank = owner_rank.at[:, :, :, 0].set(jnp.where(forced, 0, owner_rank[:, :, :, 0]))
    choose = choose.at[:, :, :, 0].set(jnp.where(forced, sample_ids % CAP, choose[:, :, :, 0]))
    group_ids = jnp.arange(groups, dtype=jnp.int32)[:, None, None, None]
    table_ids = jnp.arange(NT, dtype=jnp.int32)[None, None, :, None]
    owner = owner_order[group_ids, table_ids, owner_rank]
    local = picks[group_ids, table_ids, owner, choose]
    return (owner * ROWS_DEV + local).reshape(BATCH, NT, MAXBAG).astype(jnp.int32)


def with_ends(entries, own_key, least, top_value):
    index_at = [jax.random.randint(jax.random.fold_in(own_key, axis), (), 0, length) for axis, length in enumerate(entries.shape)]
    widest = entries.shape.index(max(entries.shape))
    neighbour = index_at[:widest] + [(index_at[widest] + 1) % entries.shape[widest]] + index_at[widest + 1:]
    return entries.at[tuple(index_at)].set(least).at[tuple(neighbour)].set(top_value)


def block_scale(own_key, shape, shards, least, top_value):
    level = 1.0
    for position, blocks in shards:
        steps = jax.random.uniform(jax.random.fold_in(jax.random.fold_in(own_key, 6), position), (blocks,), jnp.float32, least / len(shards), top_value / len(shards))
        level = level * jnp.repeat(jnp.exp(steps), shape[position] // blocks).reshape((-1,) + (1,) * (len(shape) - 1 - position))
    return level


def centred(key, dims, scale, most, shards=(), held_as=jnp.bfloat16):
    entries = scale * jax.random.normal(key, dims, jnp.float32)
    if shards:
        entries = entries * block_scale(key, dims, shards, -0.22, 0.18)
    return jnp.clip(entries, -most, most).astype(held_as)


def setup_inputs(seed: int = 0) -> dict:
    streams_of = jax.random.split(jax.random.key(seed), 12)
    return {
        "dense_input": centred(streams_of[0], (BATCH, E), 1.0, 6.0, ((0, 128),)),
        "bag_rows": draw_bag_rows(jax.random.fold_in(streams_of[11], 71), 0),
        "bag_lengths": with_ends(jax.random.randint(streams_of[2], (BATCH, NT), 1, MAXBAG + 1), jax.random.fold_in(streams_of[2], 1), 1, MAXBAG).astype(jnp.int32),
        "bag_weights": jnp.clip(jnp.exp(math.log(2.0) - 1.3862944 * jax.random.uniform(streams_of[3], (BATCH, NT, MAXBAG), jnp.float32) ** block_scale(streams_of[3], (BATCH, NT, MAXBAG), ((0, 128),), -0.2, 0.2)), 0.5, 2.0).astype(jnp.bfloat16),
        "labels": with_ends((jax.random.randint(streams_of[4], (BATCH,), 0, 4) < 1).astype(jnp.int32), jax.random.fold_in(streams_of[4], 1), 0, 1),
        "embedding": centred(streams_of[5], (ROWS, NT, E), 0.3, 2.0, ((0, 64),), jnp.float32),
        "first_moment": centred(streams_of[6], (ROWS, NT, E), 1.0, 6.0, ((0, 64),), jnp.float32),
        "second_moment": jnp.clip(jnp.exp(math.log(8.0) - 2.7725887 * jax.random.uniform(streams_of[7], (ROWS, NT), jnp.float32) ** block_scale(streams_of[7], (ROWS, NT), ((0, 64),), -0.2, 0.2)), 0.5, 8.0),
        "cross_weight": centred(streams_of[8], (D0, D0), D0 ** -0.5, 0.21875),
        "hidden_weight": centred(streams_of[9], (D0, HID), D0 ** -0.5, 0.21875),
        "head_weight": centred(streams_of[10], (HID,), HID ** -0.5, 0.09375),
    }


loss_scale = 64.0
beta_first = 0.9
beta_second = 0.99
epsilon = 1e-08

def dense_pass(dense_part, pooled, marks, cross_weight, hidden_weight, head_weight):
    samples = dense_part.shape[0]
    joined = jnp.concatenate([dense_part.astype(jnp.float32), pooled.reshape(samples, -1)], axis=1).astype(jnp.bfloat16)
    widened = joined.astype(jnp.float32)
    crossed = jnp.dot(joined, cross_weight, preferred_element_type=jnp.float32)
    layered = (widened * crossed + widened).astype(jnp.bfloat16)
    before = jnp.dot(layered, hidden_weight, preferred_element_type=jnp.float32)
    hidden = jnp.maximum(before, 0.0).astype(jnp.bfloat16)
    logits = jnp.dot(hidden, head_weight, preferred_element_type=jnp.float32)
    slope = (jax.nn.sigmoid(logits) - marks.astype(jnp.float32)) * loss_scale
    back_hidden = jnp.where(before > 0.0, slope[:, None] * head_weight.astype(jnp.float32)[None, :], 0.0).astype(jnp.bfloat16)
    back_layered = lax.dot_general(back_hidden, hidden_weight, (((1,), (1,)), ((), ())), preferred_element_type=jnp.float32)
    mixed = (back_layered * widened).astype(jnp.bfloat16)
    back_joined = back_layered * (crossed + 1.0) + lax.dot_general(mixed, cross_weight, (((1,), (1,)), ((), ())), preferred_element_type=jnp.float32)
    return back_joined[:, dense_part.shape[1]:].reshape(pooled.shape).astype(jnp.bfloat16)

def adam_rows(row_grad, hits, first_moment, second_moment):
    touched = hits > 0.0
    first_new = jnp.where(touched[:, :, None], beta_first * first_moment + (1.0 - beta_first) * row_grad, first_moment)
    second_new = jnp.where(touched, beta_second * second_moment + (1.0 - beta_second) * lax.optimization_barrier(jnp.mean(row_grad * row_grad, axis=2)), second_moment)
    step = jnp.where(touched[:, :, None], first_new / (jnp.sqrt(second_new)[:, :, None] + epsilon), 0.0)
    return (first_new, second_new, step)

def first_coefficients(bags, masses, usable):
    slots = bags.shape[2]
    slot_ids = jnp.arange(slots, dtype=jnp.int32)
    same = bags[:, :, :, None] == bags[:, :, None, :]
    summed = lax.optimization_barrier(jnp.sum(jnp.where(same, masses[:, :, None, :], 0.0), axis=3))
    earlier = same & usable[:, :, None, :] & (slot_ids[None, :] < slot_ids[:, None])[None, None, :, :]
    first = usable & jnp.logical_not(jnp.any(earlier, axis=3))
    rounded = lax.optimization_barrier(summed.astype(jnp.bfloat16))
    return jnp.where(first, rounded.astype(jnp.float32), 0.0)

def reference(dense_input, bag_rows, bag_lengths, bag_weights, labels, embedding, first_moment, second_moment, cross_weight, hidden_weight, head_weight):
    embedding_low = embedding.astype(jnp.bfloat16)
    group = B_DEV * N_SHARD
    tables = embedding.shape[1]
    width = embedding.shape[2]
    total_rows = embedding.shape[0]
    blocks = (dense_input.reshape(N_REPLICA, group, width), bag_rows.reshape(N_REPLICA, group, tables, -1), bag_lengths.reshape(N_REPLICA, group, tables), bag_weights.reshape(N_REPLICA, group, tables, -1), labels.reshape(N_REPLICA, group))

    def one_replica(carry, block):
        dense_part, bags, lengths, weights, marks = block
        slot_ids = jnp.arange(bags.shape[2], dtype=jnp.int32)
        usable = slot_ids[None, None, :] < lengths[:, :, None]
        masses = jnp.where(usable, weights.astype(jnp.float32), 0.0)
        slot_coef = first_coefficients(bags, masses, usable)
        pooled_list = []
        for which in range(tables):
            fetched = jnp.take(embedding_low[:, which, :], bags[:, which, :], axis=0).astype(jnp.float32)
            pooled_list.append(lax.optimization_barrier(jnp.sum(slot_coef[:, which, :, None] * fetched, axis=1)))
        pooled = jnp.stack(pooled_list, axis=1)
        bag_grads = dense_pass(dense_part, pooled, marks, cross_weight, hidden_weight, head_weight)
        grad_list = []
        count_list = []
        for which in range(tables):
            spread = slot_coef[:, which, :, None] * bag_grads[:, which, None, :].astype(jnp.float32)
            flat_ids = bags[:, which, :].reshape(-1)
            grad_list.append(jax.ops.segment_sum(spread.reshape(-1, width), flat_ids, num_segments=total_rows))
            count_list.append(jax.ops.segment_sum(usable[:, which, :].reshape(-1).astype(jnp.float32), flat_ids, num_segments=total_rows))
        row_grad = jnp.stack(grad_list, axis=1)
        hits = jnp.stack(count_list, axis=1)
        first_new, second_new, step = adam_rows(row_grad, hits, first_moment, second_moment)
        return ((carry[0] + first_new, carry[1] + second_new, carry[2] + step), None)
    start = (jnp.zeros(first_moment.shape, jnp.float32), jnp.zeros(second_moment.shape, jnp.float32), jnp.zeros(first_moment.shape, jnp.float32))
    sums, _ = lax.scan(one_replica, start, blocks)
    return (sums[0] / N_REPLICA, sums[1] / N_REPLICA, sums[2] / N_REPLICA)
```

```python
import functools

import jax
import jax.numpy as jnp
from jax import lax
from jax.experimental import pallas as pl
from jax.experimental.pallas import tpu as pltpu
from jax.sharding import PartitionSpec as P

loss_scale = 64.0
beta_first = 0.9
beta_second = 0.99
epsilon = 1e-08

CAP = 32
LANES = 128
UNTOUCHED = 1e30
F32 = jnp.float32
BF16 = jnp.bfloat16
VMEM_LIMIT = 56 * 1024 * 1024

NN = (((1,), (0,)), ((), ()))
NT = (((1,), (1,)), ((), ()))
TN = (((0,), (0,)), ((), ()))


def dot(a, b, dims=NN):
    return lax.dot_general(a, b, dims, preferred_element_type=F32)


def iota(shape, axis, dtype=jnp.int32):
    return lax.broadcasted_iota(dtype, shape, axis)


def ones_where(mask):
    return jnp.where(mask, 1.0, 0.0).astype(BF16)


def index_kernel(owners, own_rows, rows_ref, lens_ref, w_ref, code_ref, ct_ref, own_hot, row_hot):
    tables, slots, samples = rows_ref.shape
    shift = own_rows.bit_length() - 1
    pieces = own_rows // LANES
    before = ones_where(iota((own_rows, own_rows), 0) < iota((own_rows, own_rows), 1))
    owner_ids = iota((owners, samples), 0)
    row_ids = iota((own_rows, samples), 0)
    chunk = 256
    chunk_ids = iota((chunk, samples), 0)
    for t in range(tables):
        rows = rows_ref[t]
        own = rows >> shift
        loc = rows & (own_rows - 1)
        usable = iota((slots, samples), 0) < lens_ref[t : t + 1, :]
        mass = jnp.where(usable, w_ref[t].astype(F32), 0.0)
        own_used = jnp.where(usable, own, -1)
        for l in range(slots):
            cols = slice(l * samples, (l + 1) * samples)
            own_hot[:, cols] = ones_where(owner_ids == own_used[l : l + 1, :])
            row_hot[:, cols] = ones_where(row_ids == loc[l : l + 1, :])
        present = dot(own_hot[...], row_hot[...], NT) > 0.0
        rank = dot(ones_where(present), before)
        code = jnp.where(present, rank, -1.0)
        for c in range(pieces):
            code_ref[:, t * pieces + c, :] = code[:, c * LANES : (c + 1) * LANES]
        look = dot(rank.astype(BF16), row_hot[...])
        spots = []
        for l in range(slots):
            cols = slice(l * samples, (l + 1) * samples)
            found = jnp.where(owner_ids == own_used[l : l + 1, :], look[:, cols], 0.0)
            rank_l = jnp.sum(found, axis=0, keepdims=True).astype(jnp.int32)
            spots.append(own[l : l + 1, :] * CAP + rank_l)

        def fill(step, _, t=t, spots=spots, mass=mass):
            base = pl.multiple_of(step * chunk, chunk)
            acc = jnp.zeros((chunk, samples), F32)
            for l in range(slots):
                acc = acc + jnp.where(chunk_ids == spots[l] - base, mass[l : l + 1, :], 0.0)
            ct_ref[t, pl.ds(base, chunk), :] = acc.astype(BF16)
            return 0

        lax.fori_loop(0, owners * CAP // chunk, fill, 0)


def fill_hot(code_ref, hot, t, first, count, pieces):
    rank_ids = iota((CAP, LANES), 0).astype(F32)
    for d in range(count):
        codes = code_ref[first + d].astype(F32)
        for c in range(pieces):
            at = t * pieces + c
            hot[d * CAP : (d + 1) * CAP, c * LANES : (c + 1) * LANES] = ones_where(
                rank_ids == codes[at : at + 1, :]
            )


def fetch_kernel(tables, code_ref, emb_ref, out_ref, low, hot):
    devices = code_ref.shape[0]
    pieces = code_ref.shape[1] // tables
    own_rows = low.shape[1]
    halves = low.shape[2] // LANES
    for t in range(tables):
        for h in range(halves):
            at = h * tables + t
            low[t, :, h * LANES : (h + 1) * LANES] = emb_ref[
                pl.ds(at, own_rows, stride=tables * halves), :
            ].astype(BF16)
    group = hot.shape[0] // CAP

    def body(step, _):
        first = step * group
        for t in range(tables):
            fill_hot(code_ref, hot, t, first, group, pieces)
            got = dot(hot[...], low[t]).astype(BF16)
            out_ref[pl.ds(first, group), t * CAP : (t + 1) * CAP, :] = got.reshape(group, CAP, -1)
        return 0

    lax.fori_loop(0, devices // group, body, 0)


def dense_kernel(
    ct_ref, got_ref, dense_ref, labels_ref, head_ref, cross_hbm, hidden_hbm, out_ref,
    cross, hidden_w, joined, before, sems,
):
    tables, spots, samples = ct_ref.shape
    owners = spots // CAP
    width = dense_ref.shape[1]
    copy_cross = pltpu.make_async_copy(cross_hbm, cross, sems.at[0])
    copy_hidden = pltpu.make_async_copy(hidden_hbm, hidden_w, sems.at[1])
    copy_cross.start()
    copy_hidden.start()
    joined[:, :width] = dense_ref[...]
    for t in range(tables):
        got = got_ref[:, t * CAP : (t + 1) * CAP, :].reshape(spots, width)
        joined[:, (t + 1) * width : (t + 2) * width] = dot(ct_ref[t], got, TN).astype(BF16)
    copy_cross.wait()
    widened = joined[...].astype(F32)
    crossed = dot(joined[...], cross[...])
    layered = (widened * crossed + widened).astype(BF16)
    copy_hidden.wait()
    units = hidden_w.shape[1]
    chunk = 512
    logits = jnp.zeros((samples, 1), F32)
    for n in range(units // chunk):
        cols = slice(n * chunk, (n + 1) * chunk)
        part = dot(layered, hidden_w[:, cols])
        before[:, cols] = part
        active = jnp.maximum(part, 0.0).astype(BF16).astype(F32)
        logits = logits + jnp.sum(active * head_ref[:, cols], axis=1, keepdims=True)
    diagonal = iota((samples, samples), 0) == iota((samples, samples), 1)
    marks = jnp.sum(
        jnp.where(diagonal, labels_ref[...].astype(F32), 0.0), axis=1, keepdims=True
    )
    slope = (jax.nn.sigmoid(logits) - marks) * loss_scale
    back = jnp.zeros((samples, layered.shape[1]), F32)
    for n in range(units // chunk):
        cols = slice(n * chunk, (n + 1) * chunk)
        grad = jnp.where(before[:, cols] > 0.0, slope * head_ref[:, cols], 0.0).astype(BF16)
        back = back + dot(grad, hidden_w[:, cols], NT)
    mixed = (back * widened).astype(BF16)
    for t in range(tables):
        cols = slice((t + 1) * width, (t + 2) * width)
        total = back[:, cols] * (crossed[:, cols] + 1.0) + dot(mixed, cross[cols, :], NT)
        grads = total.astype(BF16)
        share = dot(ct_ref[t], grads).astype(BF16)
        out_ref[:, t * CAP : (t + 1) * CAP, :] = share.reshape(owners, CAP, width)


def collect_kernel(tables, code_ref, share_ref, out_ref, hot):
    devices = code_ref.shape[0]
    pieces = code_ref.shape[1] // tables
    own_rows = out_ref.shape[1]
    width = out_ref.shape[2]
    top = code_ref[0].astype(F32)
    for d in range(1, devices):
        top = jnp.maximum(top, code_ref[d].astype(F32))
    top = jnp.transpose(top)
    for t in range(tables):
        fill_hot(code_ref, hot, t, 0, devices, pieces)
        shares = share_ref[:, t * CAP : (t + 1) * CAP, :].reshape(devices * CAP, width)
        for c in range(pieces):
            grad = dot(hot[:, c * LANES : (c + 1) * LANES], shares, TN)
            at = t * pieces + c
            out_ref[t, c * LANES : (c + 1) * LANES, :] = jnp.where(
                top[:, at : at + 1] >= 0.0, grad, UNTOUCHED
            )


def adam_kernel(mine_ref, peer_ref, first_ref, second_ref, first_out, second_out, step_out, tall):
    tables, own_rows, width = mine_ref.shape
    pieces = own_rows // LANES
    halves = width // LANES
    for t in range(tables):
        for c in range(pieces):
            tall[t * pieces + c : t * pieces + c + 1, :] = second_ref[
                t : t + 1, c * LANES : (c + 1) * LANES
            ]
    second_all = jnp.transpose(tall[...])
    for t in range(tables):
        for c in range(pieces):
            at = t * pieces + c
            rows = slice(c * LANES, (c + 1) * LANES)
            second = second_all[:, at : at + 1]
            begin = c * LANES * tables * halves
            views = [
                pl.ds(begin + h * tables + t, LANES, stride=tables * halves) for h in range(halves)
            ]
            first = jnp.concatenate([first_ref[v, :] for v in views], axis=1)
            first_sum = 0.0
            second_sum = 0.0
            step_sum = 0.0
            for ref in (mine_ref, peer_ref):
                grad = ref[t, rows, :]
                touched = grad < UNTOUCHED
                touched_row = touched[:, :1]
                grown = beta_second * second + (1.0 - beta_second) * jnp.mean(
                    grad * grad, axis=1, keepdims=True
                )
                second_new = jnp.where(grad[:, :1] < UNTOUCHED, grown, second)
                first_new = jnp.where(
                    touched, beta_first * first + (1.0 - beta_first) * grad, first
                )
                step = jnp.where(touched, first_new / (jnp.sqrt(second_new) + epsilon), 0.0)
                first_sum = first_sum + first_new
                second_sum = second_sum + second_new
                step_sum = step_sum + step
            first_sum = first_sum * 0.5
            step_sum = step_sum * 0.5
            for h, v in enumerate(views):
                first_out[v, :] = first_sum[:, h * LANES : (h + 1) * LANES]
                step_out[v, :] = step_sum[:, h * LANES : (h + 1) * LANES]
            tall[at : at + 1, :] = jnp.transpose(
                jnp.broadcast_to(second_sum * 0.5, (LANES, LANES))
            )[:1, :]
    for t in range(tables):
        for c in range(pieces):
            at = t * pieces + c
            second_out[t : t + 1, c * LANES : (c + 1) * LANES] = tall[at : at + 1, :]


def to_rows(x):
    rows, tables, width = x.shape
    split = x.reshape(rows, tables, width // LANES, LANES)
    return jnp.transpose(split, (0, 2, 1, 3)).reshape(-1, LANES)


def from_rows(x, rows, tables, width):
    split = x.reshape(rows, width // LANES, tables, LANES)
    return jnp.transpose(split, (0, 2, 1, 3)).reshape(rows, tables, width)


def call(body, out_shape, scratch, *operands, in_hbm=()):
    vmem = pl.BlockSpec(memory_space=pltpu.VMEM)
    hbm = pl.BlockSpec(memory_space=pl.ANY)
    single = not isinstance(out_shape, tuple)
    return pl.pallas_call(
        body,
        out_shape=out_shape,
        in_specs=[hbm if n in in_hbm else vmem for n in range(len(operands))],
        out_specs=vmem if single else tuple(vmem for _ in out_shape),
        scratch_shapes=scratch,
        compiler_params=pltpu.CompilerParams(vmem_limit_bytes=VMEM_LIMIT),
    )(*operands)


def local(
    owners,
    replicas,
    dense_input,
    bag_rows,
    bag_lengths,
    bag_weights,
    labels,
    embedding,
    first_moment,
    second_moment,
    cross_weight,
    hidden_weight,
    head_weight,
):
    samples, tables, slots = bag_rows.shape
    own_rows, _, width = embedding.shape
    pieces = own_rows // LANES
    shape = jax.ShapeDtypeStruct
    code, ct = call(
        functools.partial(index_kernel, owners, own_rows),
        (
            shape((owners, tables * pieces, LANES), F32),
            shape((tables, owners * CAP, samples), BF16),
        ),
        [
            pltpu.VMEM((owners, slots * samples), BF16),
            pltpu.VMEM((own_rows, slots * samples), BF16),
        ],
        jnp.transpose(bag_rows, (1, 2, 0)),
        jnp.transpose(bag_lengths),
        jnp.transpose(bag_weights, (1, 2, 0)),
    )
    asked = lax.all_to_all(code.astype(BF16), "shard", 0, 0, tiled=True)
    found = call(
        functools.partial(fetch_kernel, tables),
        shape((owners, tables * CAP, width), BF16),
        [
            pltpu.VMEM((tables, own_rows, width), BF16),
            pltpu.VMEM((8 * CAP, own_rows), BF16),
        ],
        asked,
        to_rows(embedding),
    )
    got = lax.all_to_all(found, "shard", 0, 0, tiled=True)
    share = call(
        dense_kernel,
        shape((owners, tables * CAP, width), BF16),
        [
            pltpu.VMEM(cross_weight.shape, BF16),
            pltpu.VMEM(hidden_weight.shape, BF16),
            pltpu.VMEM((samples, cross_weight.shape[0]), BF16),
            pltpu.VMEM((samples, hidden_weight.shape[1]), F32),
            pltpu.SemaphoreType.DMA((2,)),
        ],
        ct,
        got,
        dense_input,
        labels.reshape(1, samples),
        head_weight.astype(F32).reshape(1, -1),
        cross_weight,
        hidden_weight,
        in_hbm=(5, 6),
    )
    shares = lax.all_to_all(share, "shard", 0, 0, tiled=True)
    mine = call(
        functools.partial(collect_kernel, tables),
        shape((tables, own_rows, width), F32),
        [pltpu.VMEM((owners * CAP, own_rows), BF16)],
        asked,
        shares,
    )
    peer = lax.ppermute(mine, "replica", [(0, 1), (1, 0)])
    first, second, step = call(
        adam_kernel,
        (
            shape((own_rows * tables * width // LANES, LANES), F32),
            shape((tables, own_rows), F32),
            shape((own_rows * tables * width // LANES, LANES), F32),
        ),
        [pltpu.VMEM((tables * pieces, LANES), F32)],
        mine,
        peer,
        to_rows(first_moment),
        jnp.transpose(second_moment),
    )
    return (
        from_rows(first, own_rows, tables, width),
        jnp.transpose(second),
        from_rows(step, own_rows, tables, width),
    )


def solution(mesh):
    placed = (
        P(("replica", "shard"), None),
        P(("replica", "shard"), None, None),
        P(("replica", "shard"), None),
        P(("replica", "shard"), None, None),
        P(("replica", "shard")),
        P("shard", None, None),
        P("shard", None, None),
        P("shard", None),
        P(),
        P(),
        P(),
    )
    return jax.shard_map(
        functools.partial(local, mesh.shape["shard"], mesh.shape["replica"]),
        mesh=mesh,
        in_specs=placed,
        out_specs=(P("shard", None, None), P("shard", None), P("shard", None, None)),
        check_vma=False,
    )
```

```python
import functools

import jax
import jax.numpy as jnp
from jax import lax
from jax.experimental import pallas as pl
from jax.experimental.pallas import tpu as pltpu
from jax.sharding import PartitionSpec as P

loss_scale = 64.0
beta_first = 0.9
beta_second = 0.99
epsilon = 1e-08

CAP = 32
LANES = 128
GROUP = 8
F32 = jnp.float32
BF16 = jnp.bfloat16
HOT = jnp.float8_e4m3fn
MIB = 1024 * 1024

NN = (((1,), (0,)), ((), ()))
NT = (((1,), (1,)), ((), ()))
TN = (((0,), (0,)), ((), ()))


def dot(a, b, dims=NN):
    return lax.dot_general(a, b, dims, preferred_element_type=F32)


def iota(shape, axis, dtype=jnp.int32):
    return lax.broadcasted_iota(dtype, shape, axis)


def ones_where(mask):
    return jnp.where(mask, 1.0, 0.0).astype(BF16)


def matches(ids, row):
    wanted = jnp.broadcast_to(row, ids.shape).astype(BF16)
    return jnp.where(ids == wanted, jnp.ones_like(ids), jnp.zeros_like(ids))


def fill_row_hot(row_hot, l, row):
    own_rows = row_hot.shape[0]
    samples = row.shape[1]
    block = 256
    ids = iota((block, samples), 0).astype(F32).astype(BF16)
    for n in range(own_rows // block):
        inside = row - n * block
        inside = jnp.where((inside >= 0.0) & (inside < block), inside, -1.0)
        row_hot[n * block : (n + 1) * block, l * samples : (l + 1) * samples] = matches(ids, inside)


def index_kernel(owners, own_rows, rows_ref, lens_ref, code_ref, rank_ref, own_hot, row_hot, wide):
    tables, slots, samples = rows_ref.shape
    shift = own_rows.bit_length() - 1
    pieces = own_rows // LANES
    before = ones_where(iota((own_rows, own_rows), 0) < iota((own_rows, own_rows), 1))
    owner_ids = iota((owners, samples), 0)
    for t in range(tables):
        rows = rows_ref[t]
        usable = iota((slots, samples), 0) < lens_ref[t : t + 1, :]
        own = jnp.where(usable, rows >> shift, -1)
        loc = (rows & (own_rows - 1)).astype(F32)
        for l in range(slots):
            cols = slice(l * samples, (l + 1) * samples)
            own_hot[:, cols] = ones_where(owner_ids == own[l : l + 1, :])
            fill_row_hot(row_hot, l, loc[l : l + 1, :])
        present = dot(own_hot[...], row_hot[...], NT) > 0.0
        rank = dot(ones_where(present), before)
        code = jnp.where(present, rank, -1.0)
        for c in range(pieces):
            wide[:, t * pieces + c, :] = code[:, c * LANES : (c + 1) * LANES]
        rank_ref[t] = rank.astype(BF16)
    code_ref[...] = wide[...].astype(BF16)


def weigh_kernel(rows_ref, lens_ref, w_ref, rank_ref, ct_ref, row_hot):
    tables, slots, samples = rows_ref.shape
    owners, own_rows = rank_ref.shape[1:]
    shift = own_rows.bit_length() - 1
    owner_ids = iota((owners, samples), 0)
    chunk = 256
    chunk_ids = iota((chunk, samples), 0)
    for t in range(tables):
        rows = rows_ref[t]
        own = rows >> shift
        loc = (rows & (own_rows - 1)).astype(F32)
        usable = iota((slots, samples), 0) < lens_ref[t : t + 1, :]
        mass = jnp.where(usable, w_ref[t].astype(F32), 0.0)
        for l in range(slots):
            fill_row_hot(row_hot, l, loc[l : l + 1, :])
        look = dot(rank_ref[t], row_hot[...])
        spots = []
        for l in range(slots):
            cols = slice(l * samples, (l + 1) * samples)
            found = jnp.where(owner_ids == own[l : l + 1, :], look[:, cols], 0.0)
            rank_l = jnp.sum(found, axis=0, keepdims=True).astype(jnp.int32)
            spots.append(own[l : l + 1, :] * CAP + rank_l)

        def fill(step, _, t=t, spots=spots, mass=mass):
            base = pl.multiple_of(step * chunk, chunk)
            acc = jnp.zeros((chunk, samples), F32)
            for l in range(slots):
                acc = acc + jnp.where(chunk_ids == spots[l] - base, mass[l : l + 1, :], 0.0)
            ct_ref[t, pl.ds(base, chunk), :] = acc.astype(BF16)
            return 0

        lax.fori_loop(0, owners * CAP // chunk, fill, 0)


def hot_rows(codes, rank_ids, t, pieces):
    return [
        matches(rank_ids, codes[t * pieces + c : t * pieces + c + 1, :])
        for c in range(pieces)
    ]


def low_kernel(tables, emb_ref, low_ref):
    own_rows, width = low_ref.shape[1:]
    halves = width // LANES
    for t in range(tables):
        for h in range(halves):
            view = pl.ds(h * tables + t, own_rows, stride=tables * halves)
            low_ref[t, :, h * LANES : (h + 1) * LANES] = emb_ref[view, :].astype(BF16)


def fetch_kernel(code_ref, low_ref, out_hbm, hot, out, sems):
    devices = code_ref.shape[0]
    tables = low_ref.shape[0]
    pieces = code_ref.shape[1] // tables
    group = hot.shape[1] // CAP
    rank_ids = iota((CAP, LANES), 0).astype(F32).astype(BF16)

    def body(step, _):
        first = step * group
        for d in range(group):
            codes = code_ref[first + d].astype(F32)
            for t in range(tables):
                for c, part in enumerate(hot_rows(codes, rank_ids, t, pieces)):
                    hot[t, d * CAP : (d + 1) * CAP, c * LANES : (c + 1) * LANES] = part
        for t in range(tables):
            got = dot(hot[t], low_ref[t]).astype(BF16)
            out[pl.ds(first, group), t * CAP : (t + 1) * CAP, :] = got.reshape(group, CAP, -1)
        send(step).start()
        return 0

    def send(step):
        block = pl.ds(step * group, group)
        return pltpu.make_async_copy(out.at[block], out_hbm.at[block], sems.at[step])

    steps = devices // group
    lax.fori_loop(0, steps, body, 0)
    for step in range(steps):
        send(step).wait()


def dense_kernel(
    ct_ref, got_ref, dense_ref, labels_ref, head_ref, cross_hbm, hidden_hbm, out_hbm,
    cross, hidden_w, joined, before, out, sems, out_sems,
):
    tables, spots, samples = ct_ref.shape
    owners = spots // CAP
    width = dense_ref.shape[1]
    copy_cross = pltpu.make_async_copy(cross_hbm, cross, sems.at[0])
    copy_hidden = pltpu.make_async_copy(hidden_hbm, hidden_w, sems.at[1])
    copy_cross.start()
    copy_hidden.start()
    joined[:, :width] = dense_ref[...]
    for t in range(tables):
        got = got_ref[:, t * CAP : (t + 1) * CAP, :].reshape(spots, width)
        joined[:, (t + 1) * width : (t + 2) * width] = dot(ct_ref[t], got, TN).astype(BF16)
    copy_cross.wait()
    widened = joined[...].astype(F32)
    crossed = dot(joined[...], cross[...])
    layered = (widened * crossed + widened).astype(BF16)
    copy_hidden.wait()
    units = hidden_w.shape[1]
    chunk = 512
    logits = jnp.zeros((samples, 1), F32)
    for n in range(units // chunk):
        cols = slice(n * chunk, (n + 1) * chunk)
        part = dot(layered, hidden_w[:, cols])
        before[:, cols] = part
        active = jnp.maximum(part, 0.0).astype(BF16).astype(F32)
        logits = logits + jnp.sum(active * head_ref[:, cols], axis=1, keepdims=True)
    diagonal = iota((samples, samples), 0) == iota((samples, samples), 1)
    marks = jnp.sum(
        jnp.where(diagonal, labels_ref[...].astype(F32), 0.0), axis=1, keepdims=True
    )
    slope = (jax.nn.sigmoid(logits) - marks) * loss_scale
    back = jnp.zeros((samples, layered.shape[1]), F32)
    for n in range(units // chunk):
        cols = slice(n * chunk, (n + 1) * chunk)
        grad = jnp.where(before[:, cols] > 0.0, slope * head_ref[:, cols], 0.0).astype(BF16)
        back = back + dot(grad, hidden_w[:, cols], NT)
    mixed = (back * widened).astype(BF16)
    steps = out_sems.shape[0]
    part_rows = spots // steps
    part_owners = owners // steps

    def send(n):
        block = pl.ds(n * part_owners, part_owners)
        return pltpu.make_async_copy(out.at[block], out_hbm.at[block], out_sems.at[n])

    for t in range(tables):
        cols = slice((t + 1) * width, (t + 2) * width)
        total = back[:, cols] * (crossed[:, cols] + 1.0) + dot(mixed, cross[cols, :], NT)
        grads = total.astype(BF16)
        for n in range(steps):
            share = dot(ct_ref[t, n * part_rows : (n + 1) * part_rows, :], grads).astype(BF16)
            block = slice(n * part_owners, (n + 1) * part_owners)
            out[block, t * CAP : (t + 1) * CAP, :] = share.reshape(part_owners, CAP, width)
            if t == tables - 1:
                send(n).start()
    for n in range(steps):
        send(n).wait()


def spread_kernel(tables, code_ref, second_ref, hot_ref, columns_ref, tall):
    devices = code_ref.shape[0]
    pieces = code_ref.shape[1] // tables
    count = tables * pieces
    rank_ids = iota((CAP, LANES), 0).astype(F32).astype(BF16)
    group = LANES // CAP

    def body(step, top):
        first = step * group
        codes = [code_ref[first + d].astype(F32) for d in range(group)]
        for t in range(tables):
            parts = [hot_rows(code, rank_ids, t, pieces) for code in codes]
            for c in range(pieces):
                block = jnp.concatenate([part[c] for part in parts], axis=0)
                hot_ref[
                    t, c * LANES : (c + 1) * LANES, pl.ds(pl.multiple_of(step * LANES, LANES), LANES)
                ] = jnp.transpose(block).astype(HOT)
        for code in codes:
            top = jnp.maximum(top, code)
        return top

    top = lax.fori_loop(0, devices // group, body, jnp.full((count, LANES), -1.0, F32))
    tall[...] = jnp.zeros_like(tall)
    tall[:count, :] = top
    for t in range(tables):
        for c in range(pieces):
            at = count + t * pieces + c
            tall[at : at + 1, :] = second_ref[t : t + 1, c * LANES : (c + 1) * LANES]
    columns_ref[...] = jnp.transpose(tall[...])


def collect_kernel(hot_ref, columns_ref, share_ref, out_ref):
    tables, own_rows, spots = hot_ref.shape
    width = share_ref.shape[2]
    pieces = own_rows // LANES
    count = tables * pieces
    lane_ids = iota((LANES, LANES), 1)
    stats = jnp.zeros((LANES, LANES), F32)
    for t in range(tables):
        shares = share_ref[:, t * CAP : (t + 1) * CAP, :].reshape(spots, width)
        for c in range(pieces):
            at = t * pieces + c
            grad = dot(hot_ref[t, c * LANES : (c + 1) * LANES, :].astype(BF16), shares)
            touched = columns_ref[:, at : at + 1] >= 0.0
            second = columns_ref[:, count + at : count + at + 1]
            mean = jnp.mean(grad * grad, axis=1, keepdims=True)
            second = jnp.where(
                touched, beta_second * second + (1.0 - beta_second) * mean, second
            )
            scale = jnp.where(touched, 1.0 / (jnp.sqrt(second) + epsilon), 0.0)
            decay = jnp.where(touched, beta_first, 1.0)
            stats = jnp.where(lane_ids == at, second, stats)
            stats = jnp.where(lane_ids == count + at, scale, stats)
            stats = jnp.where(lane_ids == 2 * count + at, decay, stats)
            out_ref[at * LANES : (at + 1) * LANES, :] = (1.0 - beta_first) * grad
    out_ref[count * LANES :, :LANES] = stats
    out_ref[count * LANES :, LANES:] = jnp.zeros((LANES, width - LANES), F32)


def adam_kernel(mine_ref, peer_ref, first_ref, first_out, second_out, step_out):
    tables, own_rows = second_out.shape
    width = mine_ref.shape[1]
    pieces = own_rows // LANES
    halves = width // LANES
    count = tables * pieces
    mine = mine_ref[count * LANES :, :LANES]
    peer = peer_ref[count * LANES :, :LANES]
    second_all = jnp.transpose((mine + peer) * 0.5)
    for t in range(tables):
        for c in range(pieces):
            at = t * pieces + c
            rows = slice(at * LANES, (at + 1) * LANES)
            second_out[t : t + 1, c * LANES : (c + 1) * LANES] = second_all[at : at + 1, :]
            sides = [
                (
                    ref,
                    jnp.broadcast_to(s[:, 2 * count + at : 2 * count + at + 1], (LANES, LANES)),
                    jnp.broadcast_to(s[:, count + at : count + at + 1] * 0.5, (LANES, LANES)),
                )
                for ref, s in ((mine_ref, mine), (peer_ref, peer))
            ]
            for h in range(halves):
                view = pl.ds(
                    c * LANES * count // pieces * halves + h * tables + t,
                    LANES,
                    stride=tables * halves,
                )
                first = first_ref[view, :]
                cols = slice(h * LANES, (h + 1) * LANES)
                firsts = [decay * first + ref[rows, cols] for ref, decay, _ in sides]
                first_out[view, :] = (firsts[0] + firsts[1]) * 0.5
                step_out[view, :] = firsts[0] * sides[0][2] + firsts[1] * sides[1][2]


def to_rows(x):
    rows, tables, width = x.shape
    split = x.reshape(rows, tables, width // LANES, LANES)
    return jnp.transpose(split, (0, 2, 1, 3)).reshape(-1, LANES)


def from_rows(x, rows, tables, width):
    split = x.reshape(rows, width // LANES, tables, LANES)
    return jnp.transpose(split, (0, 2, 1, 3)).reshape(rows, tables, width)


def call(body, mib, out_shape, scratch, *operands, in_hbm=(), out_hbm=False):
    vmem = pl.BlockSpec(memory_space=pltpu.VMEM)
    hbm = pl.BlockSpec(memory_space=pltpu.HBM)
    single = not isinstance(out_shape, tuple)
    return pl.pallas_call(
        body,
        out_shape=out_shape,
        in_specs=[hbm if n in in_hbm else vmem for n in range(len(operands))],
        out_specs=(hbm if out_hbm else vmem) if single else tuple(vmem for _ in out_shape),
        scratch_shapes=scratch,
        compiler_params=pltpu.CompilerParams(vmem_limit_bytes=mib * MIB),
    )(*operands)


def local(
    owners,
    dense_input,
    bag_rows,
    bag_lengths,
    bag_weights,
    labels,
    embedding,
    first_moment,
    second_moment,
    cross_weight,
    hidden_weight,
    head_weight,
):
    samples, tables, slots = bag_rows.shape
    own_rows, _, width = embedding.shape
    pieces = own_rows // LANES
    count = tables * pieces
    spots = owners * CAP
    shape = jax.ShapeDtypeStruct
    rows = jnp.transpose(bag_rows, (1, 2, 0))
    lens = jnp.transpose(bag_lengths)
    code, rank = call(
        functools.partial(index_kernel, owners, own_rows),
        56,
        (
            shape((owners, count, LANES), BF16),
            shape((tables, owners, own_rows), BF16),
        ),
        [
            pltpu.VMEM((owners, slots * samples), BF16),
            pltpu.VMEM((own_rows, slots * samples), BF16),
            pltpu.VMEM((owners, count, LANES), F32),
        ],
        rows,
        lens,
    )
    asked = lax.all_to_all(code, "shard", 0, 0, tiled=True)
    low = call(
        functools.partial(low_kernel, tables),
        6,
        shape((tables, own_rows, width), BF16),
        [],
        to_rows(embedding),
    )
    found = call(
        fetch_kernel,
        50,
        shape((owners, tables * CAP, width), BF16),
        [
            pltpu.VMEM((tables, GROUP * CAP, own_rows), BF16),
            pltpu.VMEM((owners, tables * CAP, width), BF16),
            pltpu.SemaphoreType.DMA((owners // GROUP,)),
        ],
        asked,
        low,
        out_hbm=True,
    )
    got = lax.all_to_all(found, "shard", 0, 0, tiled=True)
    ct = call(
        weigh_kernel,
        12,
        shape((tables, spots, samples), BF16),
        [pltpu.VMEM((own_rows, slots * samples), BF16)],
        rows,
        lens,
        jnp.transpose(bag_weights, (1, 2, 0)),
        rank,
    )
    share = call(
        dense_kernel,
        50,
        shape((owners, tables * CAP, width), BF16),
        [
            pltpu.VMEM(cross_weight.shape, BF16),
            pltpu.VMEM(hidden_weight.shape, BF16),
            pltpu.VMEM((samples, cross_weight.shape[0]), BF16),
            pltpu.VMEM((samples, hidden_weight.shape[1]), F32),
            pltpu.VMEM((owners, tables * CAP, width), BF16),
            pltpu.SemaphoreType.DMA((2,)),
            pltpu.SemaphoreType.DMA((4,)),
        ],
        ct,
        got,
        dense_input,
        labels.reshape(1, samples),
        head_weight.astype(F32).reshape(1, -1),
        cross_weight,
        hidden_weight,
        in_hbm=(5, 6),
        out_hbm=True,
    )
    shares = lax.all_to_all(share, "shard", 0, 0, tiled=True)
    asked_later, _ = lax.optimization_barrier((asked, share))
    hot, columns = call(
        functools.partial(spread_kernel, tables),
        52,
        (shape((tables, own_rows, spots), HOT), shape((LANES, LANES), F32)),
        [pltpu.VMEM((LANES, LANES), F32)],
        asked_later,
        jnp.transpose(second_moment),
    )
    mine = call(
        collect_kernel,
        14,
        shape((count * LANES + LANES, width), F32),
        [],
        hot,
        columns,
        shares,
    )
    peer = lax.ppermute(mine, "replica", [(0, 1), (1, 0)])
    first, second, step = call(
        adam_kernel,
        12,
        (
            shape((own_rows * tables * width // LANES, LANES), F32),
            shape((tables, own_rows), F32),
            shape((own_rows * tables * width // LANES, LANES), F32),
        ),
        [],
        mine,
        peer,
        to_rows(first_moment),
    )
    return (
        from_rows(first, own_rows, tables, width),
        jnp.transpose(second),
        from_rows(step, own_rows, tables, width),
    )


def solution(mesh):
    placed = (
        P(("replica", "shard"), None),
        P(("replica", "shard"), None, None),
        P(("replica", "shard"), None),
        P(("replica", "shard"), None, None),
        P(("replica", "shard")),
        P("shard", None, None),
        P("shard", None, None),
        P("shard", None),
        P(),
        P(),
        P(),
    )
    return jax.shard_map(
        functools.partial(local, mesh.shape["shard"]),
        mesh=mesh,
        in_specs=placed,
        out_specs=(P("shard", None, None), P("shard", None), P("shard", None, None)),
        check_vma=False,
    )
```

```python
import functools

import jax
import jax.numpy as jnp
from jax import lax
from jax.experimental import pallas as pl
from jax.experimental.pallas import tpu as pltpu
from jax.sharding import PartitionSpec as P

loss_scale = 64.0
beta_first = 0.9
beta_second = 0.99
epsilon = 1e-08

CAP = 32
LANES = 128
GROUP = 8
F32 = jnp.float32
BF16 = jnp.bfloat16
HOT = jnp.float8_e4m3fn
MIB = 1024 * 1024

NN = (((1,), (0,)), ((), ()))
NT = (((1,), (1,)), ((), ()))
TN = (((0,), (0,)), ((), ()))


def dot(a, b, dims=NN):
    return lax.dot_general(a, b, dims, preferred_element_type=F32)


def iota(shape, axis, dtype=jnp.int32):
    return lax.broadcasted_iota(dtype, shape, axis)


def ones_where(mask):
    return jnp.where(mask, 1.0, 0.0).astype(BF16)


def matches(ids, row):
    wanted = jnp.broadcast_to(row, ids.shape).astype(BF16)
    return jnp.where(ids == wanted, jnp.ones_like(ids), jnp.zeros_like(ids))


def fill_row_hot(row_hot, l, row):
    own_rows = row_hot.shape[0]
    samples = row.shape[1]
    block = 256
    ids = iota((block, samples), 0).astype(F32).astype(BF16)
    for n in range(own_rows // block):
        inside = row - n * block
        inside = jnp.where((inside >= 0.0) & (inside < block), inside, -1.0)
        row_hot[n * block : (n + 1) * block, l * samples : (l + 1) * samples] = matches(ids, inside)


def index_kernel(owners, own_rows, rows_ref, lens_ref, code_ref, rank_ref, own_hot, row_hot, wide):
    tables, slots, samples = rows_ref.shape
    shift = own_rows.bit_length() - 1
    pieces = own_rows // LANES
    before = ones_where(iota((own_rows, own_rows), 0) < iota((own_rows, own_rows), 1))
    owner_ids = iota((owners, samples), 0)
    for t in range(tables):
        rows = rows_ref[t]
        usable = iota((slots, samples), 0) < lens_ref[t : t + 1, :]
        own = jnp.where(usable, rows >> shift, -1)
        loc = (rows & (own_rows - 1)).astype(F32)
        for l in range(slots):
            cols = slice(l * samples, (l + 1) * samples)
            own_hot[t, :, cols] = ones_where(owner_ids == own[l : l + 1, :])
            fill_row_hot(row_hot.at[t], l, loc[l : l + 1, :])
        present = dot(own_hot[t], row_hot[t], NT) > 0.0
        rank = dot(ones_where(present), before)
        code = jnp.where(present, rank, -1.0)
        for c in range(pieces):
            wide[:, t * pieces + c, :] = code[:, c * LANES : (c + 1) * LANES]
        rank_ref[t] = rank.astype(BF16)
    code_ref[...] = wide[...].astype(BF16)


def weigh_kernel(rows_ref, lens_ref, w_ref, rank_ref, ct_ref, row_hot):
    tables, slots, samples = rows_ref.shape
    owners, own_rows = rank_ref.shape[1:]
    shift = own_rows.bit_length() - 1
    owner_ids = iota((owners, samples), 0)
    chunk = 256
    chunk_ids = iota((chunk, samples), 0)
    for t in range(tables):
        rows = rows_ref[t]
        own = rows >> shift
        loc = (rows & (own_rows - 1)).astype(F32)
        usable = iota((slots, samples), 0) < lens_ref[t : t + 1, :]
        mass = jnp.where(usable, w_ref[t].astype(F32), 0.0)
        for l in range(slots):
            fill_row_hot(row_hot, l, loc[l : l + 1, :])
        look = dot(rank_ref[t], row_hot[...])
        spots = []
        for l in range(slots):
            cols = slice(l * samples, (l + 1) * samples)
            found = jnp.where(owner_ids == own[l : l + 1, :], look[:, cols], 0.0)
            rank_l = jnp.sum(found, axis=0, keepdims=True).astype(jnp.int32)
            spots.append(own[l : l + 1, :] * CAP + rank_l)

        def fill(step, _, t=t, spots=spots, mass=mass):
            base = pl.multiple_of(step * chunk, chunk)
            acc = jnp.zeros((chunk, samples), F32)
            for l in range(slots):
                acc = acc + jnp.where(chunk_ids == spots[l] - base, mass[l : l + 1, :], 0.0)
            ct_ref[t, pl.ds(base, chunk), :] = acc.astype(BF16)
            return 0

        lax.fori_loop(0, owners * CAP // chunk, fill, 0)


def hot_rows(codes, rank_ids, t, pieces):
    return [
        matches(rank_ids, codes[t * pieces + c : t * pieces + c + 1, :])
        for c in range(pieces)
    ]


def low_kernel(tables, emb_ref, low_ref):
    own_rows, width = low_ref.shape[1:]
    halves = width // LANES
    for t in range(tables):
        for h in range(halves):
            view = pl.ds(h * tables + t, own_rows, stride=tables * halves)
            low_ref[t, :, h * LANES : (h + 1) * LANES] = emb_ref[view, :].astype(BF16)


def fetch_kernel(code_ref, low_ref, out_hbm, hot, out, sems):
    devices = code_ref.shape[0]
    tables = low_ref.shape[0]
    pieces = code_ref.shape[1] // tables
    group = hot.shape[2] // CAP
    steps = devices // group
    rank_ids = iota((CAP, LANES), 0).astype(F32).astype(BF16)

    def send(step):
        block = pl.ds(step * group, group)
        return pltpu.make_async_copy(out.at[block], out_hbm.at[block], sems.at[step])

    for step in range(steps):
        first = step * group
        slot = hot.at[step % 2]
        for d in range(group):
            codes = code_ref[first + d].astype(F32)
            for t in range(tables):
                for c, part in enumerate(hot_rows(codes, rank_ids, t, pieces)):
                    slot[t, d * CAP : (d + 1) * CAP, c * LANES : (c + 1) * LANES] = part
        for t in range(tables):
            got = dot(slot[t], low_ref[t]).astype(BF16)
            out[first : first + group, t * CAP : (t + 1) * CAP, :] = got.reshape(group, CAP, -1)
        send(step).start()
    for step in range(steps):
        send(step).wait()


def dense_kernel(
    ct_ref, dense_ref, labels_ref, head_ref, got_hbm, cross_hbm, hidden_hbm, out_hbm,
    got, cross, hidden_w, joined, before, out_grad, out, sems, out_sems,
):
    tables, spots, samples = ct_ref.shape
    owners = spots // CAP
    width = dense_ref.shape[1]
    units = hidden_w.shape[1]
    chunk = 1024
    take_got = [
        pltpu.make_async_copy(got_hbm.at[:, pl.ds(t * CAP, CAP), :], got.at[t], sems.at[t])
        for t in range(tables)
    ]
    take_cross = pltpu.make_async_copy(cross_hbm, cross, sems.at[tables])
    take_hidden = [
        pltpu.make_async_copy(
            hidden_hbm.at[:, pl.ds(n * chunk, chunk)],
            hidden_w.at[:, pl.ds(n * chunk, chunk)],
            sems.at[tables + 1 + n],
        )
        for n in range(units // chunk)
    ]
    for copy in take_got + [take_cross] + take_hidden:
        copy.start()
    joined[:, :width] = dense_ref[...]
    for t in range(tables):
        take_got[t].wait()
        rows = got[t].reshape(spots, width)
        joined[:, (t + 1) * width : (t + 2) * width] = dot(ct_ref[t], rows, TN).astype(BF16)
    take_cross.wait()
    widened = joined[...].astype(F32)
    crossed = dot(joined[...], cross[...])
    layered = (widened * crossed + widened).astype(BF16)
    logits = jnp.zeros((samples, LANES), F32)
    for n in range(units // chunk):
        cols = slice(n * chunk, (n + 1) * chunk)
        take_hidden[n].wait()
        part = dot(layered, hidden_w[:, cols])
        before[:, cols] = part
        active = jnp.maximum(part, 0.0).astype(BF16).astype(F32)
        active = active * head_ref[:, cols]
        for m in range(chunk // LANES):
            logits = logits + active[:, m * LANES : (m + 1) * LANES]
    logits = jnp.sum(logits, axis=1, keepdims=True)
    diagonal = iota((samples, samples), 0) == iota((samples, samples), 1)
    marks = jnp.sum(
        jnp.where(diagonal, labels_ref[...].astype(F32), 0.0), axis=1, keepdims=True
    )
    slope = (jax.nn.sigmoid(logits) - marks) * loss_scale
    back = jnp.zeros((samples, layered.shape[1]), F32)
    for n in range(units // chunk):
        cols = slice(n * chunk, (n + 1) * chunk)
        out_grad[:, cols] = jnp.where(
            before[:, cols] > 0.0, slope * head_ref[:, cols], 0.0
        ).astype(BF16)
    back = dot(out_grad[...], hidden_w[...], NT)
    mixed = (back * widened).astype(BF16)
    steps = out_sems.shape[1]
    part_rows = spots // steps
    part_owners = owners // steps

    def send(t, n):
        block = (pl.ds(n * part_owners, part_owners), pl.ds(t * CAP, CAP))
        return pltpu.make_async_copy(out.at[block], out_hbm.at[block], out_sems.at[t, n])

    for t in range(tables):
        cols = slice((t + 1) * width, (t + 2) * width)
        total = back[:, cols] * (crossed[:, cols] + 1.0) + dot(mixed, cross[cols, :], NT)
        grads = total.astype(BF16)
        for n in range(steps):
            share = dot(ct_ref[t, n * part_rows : (n + 1) * part_rows, :], grads).astype(BF16)
            block = slice(n * part_owners, (n + 1) * part_owners)
            out[block, t * CAP : (t + 1) * CAP, :] = share.reshape(part_owners, CAP, width)
            send(t, n).start()
    for t in range(tables):
        for n in range(steps):
            send(t, n).wait()


def spread_kernel(tables, code_ref, second_ref, *refs):
    hot_refs, (columns_ref, tall) = refs[:tables], refs[tables:]
    devices = code_ref.shape[0]
    pieces = code_ref.shape[1] // tables
    count = tables * pieces
    rank_ids = iota((CAP, LANES), 0).astype(F32).astype(BF16)
    group = LANES // CAP

    def body(step, top):
        first = step * group
        codes = [code_ref[first + d].astype(F32) for d in range(group)]
        for t in range(tables):
            parts = [hot_rows(code, rank_ids, t, pieces) for code in codes]
            for c in range(pieces):
                block = jnp.concatenate([part[c] for part in parts], axis=0)
                hot_refs[t][
                    c * LANES : (c + 1) * LANES, pl.ds(pl.multiple_of(step * LANES, LANES), LANES)
                ] = jnp.transpose(block).astype(HOT)
        for code in codes:
            top = jnp.maximum(top, code)
        return top

    top = lax.fori_loop(0, devices // group, body, jnp.full((count, LANES), -1.0, F32))
    tall[...] = jnp.zeros_like(tall)
    tall[:count, :] = top
    for t in range(tables):
        for c in range(pieces):
            at = count + t * pieces + c
            tall[at : at + 1, :] = second_ref[t : t + 1, c * LANES : (c + 1) * LANES]
    columns_ref[...] = jnp.transpose(tall[...])


def collect_kernel(t, tables, hot_ref, columns_ref, share_ref, out_ref):
    own_rows, spots = hot_ref.shape
    width = share_ref.shape[2]
    pieces = own_rows // LANES
    lane_ids = iota((LANES, LANES), 1)
    stats = jnp.zeros((LANES, LANES), F32)
    shares = share_ref[:, t * CAP : (t + 1) * CAP, :].reshape(spots, width)
    for c in range(pieces):
        at = t * pieces + c
        grad = dot(hot_ref[c * LANES : (c + 1) * LANES, :].astype(BF16), shares)
        touched = columns_ref[:, at : at + 1] >= 0.0
        at = at + tables * pieces
        second = columns_ref[:, at : at + 1]
        mean = jnp.mean(grad * grad, axis=1, keepdims=True)
        second = jnp.where(touched, beta_second * second + (1.0 - beta_second) * mean, second)
        scale = jnp.where(touched, 1.0 / (jnp.sqrt(second) + epsilon), 0.0)
        decay = jnp.where(touched, beta_first, 1.0)
        stats = jnp.where(lane_ids == c, second, stats)
        stats = jnp.where(lane_ids == pieces + c, scale, stats)
        stats = jnp.where(lane_ids == 2 * pieces + c, decay, stats)
        out_ref[c * LANES : (c + 1) * LANES, :] = (1.0 - beta_first) * grad
    out_ref[own_rows:, :LANES] = stats
    out_ref[own_rows:, LANES:] = jnp.zeros((LANES, width - LANES), F32)


def adam_kernel(tables, *refs):
    mine_refs, peer_refs = refs[:tables], refs[tables : 2 * tables]
    first_ref, first_out, second_out, step_out = refs[2 * tables :]
    own_rows = second_out.shape[1]
    width = mine_refs[0].shape[1]
    pieces = own_rows // LANES
    halves = width // LANES
    for t in range(tables):
        pair = (mine_refs[t], peer_refs[t])
        stats = [ref[own_rows:, :LANES] for ref in pair]
        second = jnp.transpose((stats[0] + stats[1]) * 0.5)
        for c in range(pieces):
            rows = slice(c * LANES, (c + 1) * LANES)
            second_out[t : t + 1, rows] = second[c : c + 1, :]
            scales = [
                jnp.broadcast_to(s[:, pieces + c : pieces + c + 1] * 0.5, (LANES, LANES))
                for s in stats
            ]
            decays = [
                jnp.broadcast_to(s[:, 2 * pieces + c : 2 * pieces + c + 1], (LANES, LANES))
                for s in stats
            ]
            for h in range(halves):
                view = pl.ds(
                    c * LANES * tables * halves + h * tables + t, LANES, stride=tables * halves
                )
                first = first_ref[view, :]
                cols = slice(h * LANES, (h + 1) * LANES)
                firsts = [decay * first + ref[rows, cols] for decay, ref in zip(decays, pair)]
                first_out[view, :] = (firsts[0] + firsts[1]) * 0.5
                step_out[view, :] = firsts[0] * scales[0] + firsts[1] * scales[1]


def to_rows(x):
    rows, tables, width = x.shape
    split = x.reshape(rows, tables, width // LANES, LANES)
    return jnp.transpose(split, (0, 2, 1, 3)).reshape(-1, LANES)


def from_rows(x, rows, tables, width):
    split = x.reshape(rows, width // LANES, tables, LANES)
    return jnp.transpose(split, (0, 2, 1, 3)).reshape(rows, tables, width)


def call(body, mib, out_shape, scratch, *operands, in_hbm=(), out_hbm=False):
    vmem = pl.BlockSpec(memory_space=pltpu.VMEM)
    hbm = pl.BlockSpec(memory_space=pltpu.HBM)
    single = not isinstance(out_shape, tuple)
    return pl.pallas_call(
        body,
        out_shape=out_shape,
        in_specs=[hbm if n in in_hbm else vmem for n in range(len(operands))],
        out_specs=(hbm if out_hbm else vmem) if single else tuple(vmem for _ in out_shape),
        scratch_shapes=scratch,
        compiler_params=pltpu.CompilerParams(vmem_limit_bytes=mib * MIB),
    )(*operands)


def local(
    owners,
    dense_input,
    bag_rows,
    bag_lengths,
    bag_weights,
    labels,
    embedding,
    first_moment,
    second_moment,
    cross_weight,
    hidden_weight,
    head_weight,
):
    samples, tables, slots = bag_rows.shape
    own_rows, _, width = embedding.shape
    pieces = own_rows // LANES
    count = tables * pieces
    spots = owners * CAP
    shape = jax.ShapeDtypeStruct
    rows = jnp.transpose(bag_rows, (1, 2, 0))
    lens = jnp.transpose(bag_lengths)
    code, rank = call(
        functools.partial(index_kernel, owners, own_rows),
        56,
        (
            shape((owners, count, LANES), BF16),
            shape((tables, owners, own_rows), BF16),
        ),
        [
            pltpu.VMEM((tables, owners, slots * samples), BF16),
            pltpu.VMEM((tables, own_rows, slots * samples), BF16),
            pltpu.VMEM((owners, count, LANES), F32),
        ],
        rows,
        lens,
    )
    asked = lax.all_to_all(code, "shard", 0, 0, tiled=True)
    low = call(
        functools.partial(low_kernel, tables),
        6,
        shape((tables, own_rows, width), BF16),
        [],
        to_rows(embedding),
    )
    found = call(
        fetch_kernel,
        50,
        shape((owners, tables * CAP, width), BF16),
        [
            pltpu.VMEM((2, tables, GROUP * CAP, own_rows), BF16),
            pltpu.VMEM((owners, tables * CAP, width), BF16),
            pltpu.SemaphoreType.DMA((owners // GROUP,)),
        ],
        asked,
        low,
        out_hbm=True,
    )
    got = lax.all_to_all(found, "shard", 0, 0, tiled=True)
    ct = call(
        weigh_kernel,
        12,
        shape((tables, spots, samples), BF16),
        [pltpu.VMEM((own_rows, slots * samples), BF16)],
        rows,
        lens,
        jnp.transpose(bag_weights, (1, 2, 0)),
        rank,
    )
    share = call(
        dense_kernel,
        50,
        shape((owners, tables * CAP, width), BF16),
        [
            pltpu.VMEM((tables, owners, CAP, width), BF16),
            pltpu.VMEM(cross_weight.shape, BF16),
            pltpu.VMEM(hidden_weight.shape, BF16),
            pltpu.VMEM((samples, cross_weight.shape[0]), BF16),
            pltpu.VMEM((samples, hidden_weight.shape[1]), F32),
            pltpu.VMEM((samples, hidden_weight.shape[1]), BF16),
            pltpu.VMEM((owners, tables * CAP, width), BF16),
            pltpu.SemaphoreType.DMA((tables + 1 + hidden_weight.shape[1] // 1024,)),
            pltpu.SemaphoreType.DMA((tables, 4)),
        ],
        ct,
        dense_input,
        labels.reshape(1, samples),
        head_weight.astype(F32).reshape(1, -1),
        got,
        cross_weight,
        hidden_weight,
        in_hbm=(4, 5, 6),
        out_hbm=True,
    )
    shares = lax.all_to_all(share, "shard", 0, 0, tiled=True)
    asked_later, _ = lax.optimization_barrier((asked, share))
    *hots, columns = call(
        functools.partial(spread_kernel, tables),
        52,
        tuple(shape((own_rows, spots), HOT) for _ in range(tables))
        + (shape((LANES, LANES), F32),),
        [pltpu.VMEM((LANES, LANES), F32)],
        asked_later,
        jnp.transpose(second_moment),
    )
    mine, peer = [], []
    for t in range(tables):
        part = call(
            functools.partial(collect_kernel, t, tables),
            14,
            shape((own_rows + LANES, width), F32),
            [],
            hots[t],
            columns,
            shares,
        )
        mine.append(part)
        peer.append(lax.ppermute(part, "replica", [(0, 1), (1, 0)]))
    first, second, step = call(
        functools.partial(adam_kernel, tables),
        12,
        (
            shape((own_rows * tables * width // LANES, LANES), F32),
            shape((tables, own_rows), F32),
            shape((own_rows * tables * width // LANES, LANES), F32),
        ),
        [],
        *mine,
        *peer,
        to_rows(first_moment),
    )
    return (
        from_rows(first, own_rows, tables, width),
        jnp.transpose(second),
        from_rows(step, own_rows, tables, width),
    )


def solution(mesh):
    placed = (
        P(("replica", "shard"), None),
        P(("replica", "shard"), None, None),
        P(("replica", "shard"), None),
        P(("replica", "shard"), None, None),
        P(("replica", "shard")),
        P("shard", None, None),
        P("shard", None, None),
        P("shard", None),
        P(),
        P(),
        P(),
    )
    return jax.shard_map(
        functools.partial(local, mesh.shape["shard"]),
        mesh=mesh,
        in_specs=placed,
        out_specs=(P("shard", None, None), P("shard", None), P("shard", None, None)),
        check_vma=False,
    )
```

```python
import functools

import jax
import jax.numpy as jnp
from jax import lax
from jax.experimental import pallas as pl
from jax.experimental.pallas import tpu as pltpu
from jax.sharding import PartitionSpec as P

loss_scale = 64.0
beta_first = 0.9
beta_second = 0.99
epsilon = 1e-08

CAP = 32
LANES = 128
GROUP = 32
F32 = jnp.float32
BF16 = jnp.bfloat16
HOT = jnp.float8_e4m3fn
MIB = 1024 * 1024

NN = (((1,), (0,)), ((), ()))
NT = (((1,), (1,)), ((), ()))
TN = (((0,), (0,)), ((), ()))


def dot(a, b, dims=NN):
    return lax.dot_general(a, b, dims, preferred_element_type=F32)


def iota(shape, axis, dtype=jnp.int32):
    return lax.broadcasted_iota(dtype, shape, axis)


def ones_where(mask):
    return jnp.where(mask, 1.0, 0.0).astype(BF16)


def matches(ids, row):
    wanted = jnp.broadcast_to(row, ids.shape).astype(BF16)
    return jnp.where(ids == wanted, jnp.ones_like(ids), jnp.zeros_like(ids))


def fill_row_hot(row_hot, l, row):
    own_rows = row_hot.shape[0]
    samples = row.shape[1]
    block = 256
    ids = iota((block, samples), 0).astype(F32).astype(BF16)
    for n in range(own_rows // block):
        inside = row - n * block
        inside = jnp.where((inside >= 0.0) & (inside < block), inside, -1.0)
        row_hot[n * block : (n + 1) * block, l * samples : (l + 1) * samples] = matches(ids, inside)


def index_kernel(owners, own_rows, rows_ref, lens_ref, code_ref, rank_ref, own_hot, row_hot, wide):
    tables, slots, samples = rows_ref.shape
    shift = own_rows.bit_length() - 1
    pieces = own_rows // LANES
    before = ones_where(iota((own_rows, own_rows), 0) < iota((own_rows, own_rows), 1))
    owner_ids = iota((owners, samples), 0)
    block = 256
    ids = iota((samples, block), 1).astype(F32).astype(BF16)
    for t in range(tables):
        rows = rows_ref[t]
        usable = iota((slots, samples), 0) < lens_ref[t : t + 1, :]
        own = jnp.where(usable, rows >> shift, -1)
        loc = (rows & (own_rows - 1)).astype(F32)
        columns = []
        for n in range(own_rows // block):
            inside = loc - n * block
            inside = jnp.where((inside >= 0.0) & (inside < block), inside, -1.0)
            columns.append(jnp.transpose(inside))
        for l in range(slots):
            cols = slice(l * samples, (l + 1) * samples)
            own_hot[t, :, cols] = ones_where(owner_ids == own[l : l + 1, :])
            for n, column in enumerate(columns):
                wanted = jnp.broadcast_to(column[:, l : l + 1], ids.shape).astype(BF16)
                row_hot[t, cols, n * block : (n + 1) * block] = jnp.where(
                    ids == wanted, jnp.ones_like(ids), jnp.zeros_like(ids)
                )
        present = dot(own_hot[t], row_hot[t]) > 0.0
        rank = dot(ones_where(present), before)
        code = jnp.where(present, rank, -1.0)
        for c in range(pieces):
            wide[:, t * pieces + c, :] = code[:, c * LANES : (c + 1) * LANES]
        rank_ref[t] = rank.astype(BF16)
    code_ref[...] = wide[...].astype(BF16)


def weigh_kernel(rows_ref, lens_ref, w_ref, rank_ref, ct_ref, row_hot):
    tables, slots, samples = rows_ref.shape
    owners, own_rows = rank_ref.shape[1:]
    shift = own_rows.bit_length() - 1
    owner_ids = iota((owners, samples), 0)
    chunk = 256
    chunk_ids = iota((chunk, samples), 0)
    for t in range(tables):
        rows = rows_ref[t]
        own = rows >> shift
        loc = (rows & (own_rows - 1)).astype(F32)
        usable = iota((slots, samples), 0) < lens_ref[t : t + 1, :]
        mass = jnp.where(usable, w_ref[t].astype(F32), 0.0)
        for l in range(slots):
            fill_row_hot(row_hot, l, loc[l : l + 1, :])
        look = dot(rank_ref[t], row_hot[...])
        spots = []
        for l in range(slots):
            cols = slice(l * samples, (l + 1) * samples)
            found = jnp.where(owner_ids == own[l : l + 1, :], look[:, cols], 0.0)
            rank_l = jnp.sum(found, axis=0, keepdims=True).astype(jnp.int32)
            spots.append(own[l : l + 1, :] * CAP + rank_l)

        def fill(step, _, t=t, spots=spots, mass=mass):
            base = pl.multiple_of(step * chunk, chunk)
            acc = jnp.zeros((chunk, samples), F32)
            for l in range(slots):
                acc = acc + jnp.where(chunk_ids == spots[l] - base, mass[l : l + 1, :], 0.0)
            ct_ref[t, pl.ds(base, chunk), :] = acc.astype(BF16)
            return 0

        lax.fori_loop(0, owners * CAP // chunk, fill, 0)


def hot_rows(codes, rank_ids, t, pieces):
    return [
        matches(rank_ids, codes[t * pieces + c : t * pieces + c + 1, :])
        for c in range(pieces)
    ]


def low_kernel(tables, emb_ref, low_ref):
    own_rows, width = low_ref.shape[1:]
    halves = width // LANES
    for t in range(tables):
        for h in range(halves):
            view = pl.ds(h * tables + t, own_rows, stride=tables * halves)
            low_ref[t, :, h * LANES : (h + 1) * LANES] = emb_ref[view, :].astype(BF16)


def fetch_kernel(code_ref, low_ref, out_hbm, hot, out, sems):
    devices = code_ref.shape[0]
    tables = low_ref.shape[0]
    pieces = code_ref.shape[1] // tables
    group = hot.shape[2] // CAP
    steps = devices // group
    rank_ids = iota((CAP, LANES), 0).astype(F32).astype(BF16)

    def send(step):
        block = pl.ds(step * group, group)
        return pltpu.make_async_copy(out.at[block], out_hbm.at[block], sems.at[step])

    for step in range(steps):
        first = step * group
        slot = hot.at[step % 2]
        for d in range(group):
            codes = code_ref[first + d].astype(F32)
            for t in range(tables):
                for c, part in enumerate(hot_rows(codes, rank_ids, t, pieces)):
                    slot[t, d * CAP : (d + 1) * CAP, c * LANES : (c + 1) * LANES] = part
        for t in range(tables):
            got = dot(slot[t], low_ref[t]).astype(BF16)
            out[first : first + group, t * CAP : (t + 1) * CAP, :] = got.reshape(group, CAP, -1)
        send(step).start()
    for step in range(steps):
        send(step).wait()


def dense_kernel(
    ct_ref, dense_ref, labels_ref, head_ref, got_hbm, cross_hbm, hidden_hbm, out_hbm,
    got, cross, hidden_w, joined, before, out_grad, out, sems, out_sems,
):
    tables, spots, samples = ct_ref.shape
    owners = spots // CAP
    width = dense_ref.shape[1]
    units = hidden_w.shape[1]
    chunk = 1024
    take_got = [
        pltpu.make_async_copy(got_hbm.at[:, pl.ds(t * CAP, CAP), :], got.at[t], sems.at[t])
        for t in range(tables)
    ]
    take_cross = pltpu.make_async_copy(cross_hbm, cross, sems.at[tables])
    take_hidden = [
        pltpu.make_async_copy(
            hidden_hbm.at[:, pl.ds(n * chunk, chunk)],
            hidden_w.at[:, pl.ds(n * chunk, chunk)],
            sems.at[tables + 1 + n],
        )
        for n in range(units // chunk)
    ]
    for copy in take_got + [take_cross] + take_hidden:
        copy.start()
    joined[:, :width] = dense_ref[...]
    for t in range(tables):
        take_got[t].wait()
        rows = got[t].reshape(spots, width)
        joined[:, (t + 1) * width : (t + 2) * width] = dot(ct_ref[t], rows, TN).astype(BF16)
    take_cross.wait()
    widened = joined[...].astype(F32)
    crossed = dot(joined[...], cross[...])
    layered = (widened * crossed + widened).astype(BF16)
    logits = jnp.zeros((samples, LANES), F32)
    for n in range(units // chunk):
        cols = slice(n * chunk, (n + 1) * chunk)
        take_hidden[n].wait()
        part = dot(layered, hidden_w[:, cols])
        before[:, cols] = part
        active = jnp.maximum(part, 0.0).astype(BF16).astype(F32)
        active = active * head_ref[:, cols]
        for m in range(chunk // LANES):
            logits = logits + active[:, m * LANES : (m + 1) * LANES]
    logits = jnp.sum(logits, axis=1, keepdims=True)
    diagonal = iota((samples, samples), 0) == iota((samples, samples), 1)
    marks = jnp.sum(
        jnp.where(diagonal, labels_ref[...].astype(F32), 0.0), axis=1, keepdims=True
    )
    slope = (jax.nn.sigmoid(logits) - marks) * loss_scale
    back = jnp.zeros((samples, layered.shape[1]), F32)
    for n in range(units // chunk):
        cols = slice(n * chunk, (n + 1) * chunk)
        out_grad[:, cols] = jnp.where(
            before[:, cols] > 0.0, slope * head_ref[:, cols], 0.0
        ).astype(BF16)
    back = dot(out_grad[...], hidden_w[...], NT)
    mixed = (back * widened).astype(BF16)
    steps = out_sems.shape[1]
    part_rows = spots // steps
    part_owners = owners // steps

    def send(t, n):
        block = (pl.ds(n * part_owners, part_owners), pl.ds(t * CAP, CAP))
        return pltpu.make_async_copy(out.at[block], out_hbm.at[block], out_sems.at[t, n])

    for t in range(tables):
        cols = slice((t + 1) * width, (t + 2) * width)
        total = back[:, cols] * (crossed[:, cols] + 1.0) + dot(mixed, cross[cols, :], NT)
        grads = total.astype(BF16)
        for n in range(steps):
            share = dot(ct_ref[t, n * part_rows : (n + 1) * part_rows, :], grads).astype(BF16)
            block = slice(n * part_owners, (n + 1) * part_owners)
            out[block, t * CAP : (t + 1) * CAP, :] = share.reshape(part_owners, CAP, width)
            send(t, n).start()
    for t in range(tables):
        for n in range(steps):
            send(t, n).wait()


def spread_kernel(tables, code_ref, second_ref, *refs):
    hot_refs, (columns_ref, tall) = refs[:tables], refs[tables:]
    devices = code_ref.shape[0]
    pieces = code_ref.shape[1] // tables
    count = tables * pieces
    rank_ids = iota((CAP, LANES), 0).astype(F32).astype(BF16)
    group = LANES // CAP

    def body(step, top):
        first = step * group
        codes = [code_ref[first + d].astype(F32) for d in range(group)]
        for t in range(tables):
            parts = [hot_rows(code, rank_ids, t, pieces) for code in codes]
            for c in range(pieces):
                block = jnp.concatenate([part[c] for part in parts], axis=0)
                hot_refs[t][
                    c * LANES : (c + 1) * LANES, pl.ds(pl.multiple_of(step * LANES, LANES), LANES)
                ] = jnp.transpose(block).astype(HOT)
        for code in codes:
            top = jnp.maximum(top, code)
        return top

    top = lax.fori_loop(0, devices // group, body, jnp.full((count, LANES), -1.0, F32))
    tall[...] = jnp.zeros_like(tall)
    tall[:count, :] = top
    for t in range(tables):
        for c in range(pieces):
            at = count + t * pieces + c
            tall[at : at + 1, :] = second_ref[t : t + 1, c * LANES : (c + 1) * LANES]
    columns_ref[...] = jnp.transpose(tall[...])


def collect_kernel(t, tables, hot_ref, columns_ref, share_ref, out_ref):
    own_rows, spots = hot_ref.shape
    width = share_ref.shape[2]
    pieces = own_rows // LANES
    lane_ids = iota((LANES, LANES), 1)
    stats = jnp.zeros((LANES, LANES), F32)
    shares = share_ref[:, t * CAP : (t + 1) * CAP, :].reshape(spots, width)
    for c in range(pieces):
        at = t * pieces + c
        grad = dot(hot_ref[c * LANES : (c + 1) * LANES, :].astype(BF16), shares)
        touched = columns_ref[:, at : at + 1] >= 0.0
        at = at + tables * pieces
        second = columns_ref[:, at : at + 1]
        mean = jnp.mean(grad * grad, axis=1, keepdims=True)
        second = jnp.where(touched, beta_second * second + (1.0 - beta_second) * mean, second)
        scale = jnp.where(touched, 1.0 / (jnp.sqrt(second) + epsilon), 0.0)
        decay = jnp.where(touched, beta_first, 1.0)
        stats = jnp.where(lane_ids == c, second, stats)
        stats = jnp.where(lane_ids == pieces + c, scale, stats)
        stats = jnp.where(lane_ids == 2 * pieces + c, decay, stats)
        out_ref[c * LANES : (c + 1) * LANES, :] = (1.0 - beta_first) * grad
    out_ref[own_rows:, :LANES] = stats
    out_ref[own_rows:, LANES:] = jnp.zeros((LANES, width - LANES), F32)


def adam_kernel(tables, *refs):
    mine_refs, peer_refs = refs[:tables], refs[tables : 2 * tables]
    first_ref, first_out, second_out, step_out = refs[2 * tables :]
    own_rows = second_out.shape[1]
    width = mine_refs[0].shape[1]
    pieces = own_rows // LANES
    halves = width // LANES
    for t in range(tables):
        pair = (mine_refs[t], peer_refs[t])
        stats = [ref[own_rows:, :LANES] for ref in pair]
        second = jnp.transpose((stats[0] + stats[1]) * 0.5)
        for c in range(pieces):
            rows = slice(c * LANES, (c + 1) * LANES)
            second_out[t : t + 1, rows] = second[c : c + 1, :]
            scales = [
                jnp.broadcast_to(s[:, pieces + c : pieces + c + 1] * 0.5, (LANES, LANES))
                for s in stats
            ]
            decays = [
                jnp.broadcast_to(s[:, 2 * pieces + c : 2 * pieces + c + 1], (LANES, LANES))
                for s in stats
            ]
            for h in range(halves):
                view = pl.ds(
                    c * LANES * tables * halves + h * tables + t, LANES, stride=tables * halves
                )
                first = first_ref[view, :]
                cols = slice(h * LANES, (h + 1) * LANES)
                firsts = [decay * first + ref[rows, cols] for decay, ref in zip(decays, pair)]
                first_out[view, :] = (firsts[0] + firsts[1]) * 0.5
                step_out[view, :] = firsts[0] * scales[0] + firsts[1] * scales[1]


def to_rows(x):
    rows, tables, width = x.shape
    split = x.reshape(rows, tables, width // LANES, LANES)
    return jnp.transpose(split, (0, 2, 1, 3)).reshape(-1, LANES)


def from_rows(x, rows, tables, width):
    split = x.reshape(rows, width // LANES, tables, LANES)
    return jnp.transpose(split, (0, 2, 1, 3)).reshape(rows, tables, width)


def call(body, mib, out_shape, scratch, *operands, in_hbm=(), out_hbm=False):
    vmem = pl.BlockSpec(memory_space=pltpu.VMEM)
    hbm = pl.BlockSpec(memory_space=pltpu.HBM)
    single = not isinstance(out_shape, tuple)
    return pl.pallas_call(
        body,
        out_shape=out_shape,
        in_specs=[hbm if n in in_hbm else vmem for n in range(len(operands))],
        out_specs=(hbm if out_hbm else vmem) if single else tuple(vmem for _ in out_shape),
        scratch_shapes=scratch,
        compiler_params=pltpu.CompilerParams(vmem_limit_bytes=mib * MIB),
    )(*operands)


def local(
    owners,
    dense_input,
    bag_rows,
    bag_lengths,
    bag_weights,
    labels,
    embedding,
    first_moment,
    second_moment,
    cross_weight,
    hidden_weight,
    head_weight,
):
    samples, tables, slots = bag_rows.shape
    own_rows, _, width = embedding.shape
    pieces = own_rows // LANES
    count = tables * pieces
    spots = owners * CAP
    shape = jax.ShapeDtypeStruct
    rows = jnp.transpose(bag_rows, (1, 2, 0))
    lens = jnp.transpose(bag_lengths)
    code, rank = call(
        functools.partial(index_kernel, owners, own_rows),
        56,
        (
            shape((owners, count, LANES), BF16),
            shape((tables, owners, own_rows), BF16),
        ),
        [
            pltpu.VMEM((tables, owners, slots * samples), BF16),
            pltpu.VMEM((tables, slots * samples, own_rows), BF16),
            pltpu.VMEM((owners, count, LANES), F32),
        ],
        rows,
        lens,
    )
    asked = lax.all_to_all(code, "shard", 0, 0, tiled=True)
    low = call(
        functools.partial(low_kernel, tables),
        6,
        shape((tables, own_rows, width), BF16),
        [],
        to_rows(embedding),
    )
    found = call(
        fetch_kernel,
        50,
        shape((owners, tables * CAP, width), BF16),
        [
            pltpu.VMEM((2, tables, GROUP * CAP, own_rows), BF16),
            pltpu.VMEM((owners, tables * CAP, width), BF16),
            pltpu.SemaphoreType.DMA((owners // GROUP,)),
        ],
        asked,
        low,
        out_hbm=True,
    )
    got = lax.all_to_all(found, "shard", 0, 0, tiled=True)
    ct = call(
        weigh_kernel,
        12,
        shape((tables, spots, samples), BF16),
        [pltpu.VMEM((own_rows, slots * samples), BF16)],
        rows,
        lens,
        jnp.transpose(bag_weights, (1, 2, 0)),
        rank,
    )
    share = call(
        dense_kernel,
        50,
        shape((owners, tables * CAP, width), BF16),
        [
            pltpu.VMEM((tables, owners, CAP, width), BF16),
            pltpu.VMEM(cross_weight.shape, BF16),
            pltpu.VMEM(hidden_weight.shape, BF16),
            pltpu.VMEM((samples, cross_weight.shape[0]), BF16),
            pltpu.VMEM((samples, hidden_weight.shape[1]), F32),
            pltpu.VMEM((samples, hidden_weight.shape[1]), BF16),
            pltpu.VMEM((owners, tables * CAP, width), BF16),
            pltpu.SemaphoreType.DMA((tables + 1 + hidden_weight.shape[1] // 1024,)),
            pltpu.SemaphoreType.DMA((tables, 4)),
        ],
        ct,
        dense_input,
        labels.reshape(1, samples),
        head_weight.astype(F32).reshape(1, -1),
        got,
        cross_weight,
        hidden_weight,
        in_hbm=(4, 5, 6),
        out_hbm=True,
    )
    shares = lax.all_to_all(share, "shard", 0, 0, tiled=True)
    asked_later, _ = lax.optimization_barrier((asked, share))
    *hots, columns = call(
        functools.partial(spread_kernel, tables),
        52,
        tuple(shape((own_rows, spots), HOT) for _ in range(tables))
        + (shape((LANES, LANES), F32),),
        [pltpu.VMEM((LANES, LANES), F32)],
        asked_later,
        jnp.transpose(second_moment),
    )
    mine, peer = [], []
    for t in range(tables):
        part = call(
            functools.partial(collect_kernel, t, tables),
            14,
            shape((own_rows + LANES, width), F32),
            [],
            hots[t],
            columns,
            shares,
        )
        mine.append(part)
        peer.append(lax.ppermute(part, "replica", [(0, 1), (1, 0)]))
    first, second, step = call(
        functools.partial(adam_kernel, tables),
        12,
        (
            shape((own_rows * tables * width // LANES, LANES), F32),
            shape((tables, own_rows), F32),
            shape((own_rows * tables * width // LANES, LANES), F32),
        ),
        [],
        *mine,
        *peer,
        to_rows(first_moment),
    )
    return (
        from_rows(first, own_rows, tables, width),
        jnp.transpose(second),
        from_rows(step, own_rows, tables, width),
    )


def solution(mesh):
    placed = (
        P(("replica", "shard"), None),
        P(("replica", "shard"), None, None),
        P(("replica", "shard"), None),
        P(("replica", "shard"), None, None),
        P(("replica", "shard")),
        P("shard", None, None),
        P("shard", None, None),
        P("shard", None),
        P(),
        P(),
        P(),
    )
    return jax.shard_map(
        functools.partial(local, mesh.shape["shard"]),
        mesh=mesh,
        in_specs=placed,
        out_specs=(P("shard", None, None), P("shard", None), P("shard", None, None)),
        check_vma=False,
    )
```

```python
import functools

import jax
import jax.numpy as jnp
from jax import lax
from jax.experimental import pallas as pl
from jax.experimental.pallas import tpu as pltpu
from jax.sharding import PartitionSpec as P

loss_scale = 64.0
beta_first = 0.9
beta_second = 0.99
epsilon = 1e-08

CAP = 32
LANES = 128
GROUP = 32
F32 = jnp.float32
BF16 = jnp.bfloat16
HOT = jnp.float8_e4m3fn
MIB = 1024 * 1024

NN = (((1,), (0,)), ((), ()))
NT = (((1,), (1,)), ((), ()))
TN = (((0,), (0,)), ((), ()))


def dot(a, b, dims=NN):
    return lax.dot_general(a, b, dims, preferred_element_type=F32)


def iota(shape, axis, dtype=jnp.int32):
    return lax.broadcasted_iota(dtype, shape, axis)


def ones_where(mask):
    return jnp.where(mask, 1.0, 0.0).astype(BF16)


def matches(ids, row):
    wanted = jnp.broadcast_to(row, ids.shape).astype(BF16)
    return jnp.where(ids == wanted, jnp.ones_like(ids), jnp.zeros_like(ids))


def fill_row_hot(row_hot, l, row):
    own_rows = row_hot.shape[0]
    samples = row.shape[1]
    block = 256
    ids = iota((block, samples), 0).astype(F32).astype(BF16)
    for n in range(own_rows // block):
        inside = row - n * block
        inside = jnp.where((inside >= 0.0) & (inside < block), inside, -1.0)
        row_hot[n * block : (n + 1) * block, l * samples : (l + 1) * samples] = matches(ids, inside)


def index_kernel(owners, own_rows, rows_ref, lens_ref, code_ref, rank_ref, own_hot, row_hot, wide):
    tables, slots, samples = rows_ref.shape
    shift = own_rows.bit_length() - 1
    pieces = own_rows // LANES
    before = ones_where(iota((own_rows, own_rows), 0) < iota((own_rows, own_rows), 1))
    owner_ids = iota((owners, samples), 0)
    block = 256
    ids = iota((samples, block), 1).astype(F32).astype(BF16)
    for t in range(tables):
        rows = rows_ref[t]
        usable = iota((slots, samples), 0) < lens_ref[t : t + 1, :]
        own = jnp.where(usable, rows >> shift, -1)
        loc = (rows & (own_rows - 1)).astype(F32)
        columns = []
        for n in range(own_rows // block):
            inside = loc - n * block
            inside = jnp.where((inside >= 0.0) & (inside < block), inside, -1.0)
            columns.append(jnp.transpose(inside))
        for l in range(slots):
            cols = slice(l * samples, (l + 1) * samples)
            own_hot[t, :, cols] = ones_where(owner_ids == own[l : l + 1, :])
            for n, column in enumerate(columns):
                wanted = jnp.broadcast_to(column[:, l : l + 1], ids.shape).astype(BF16)
                row_hot[t, cols, n * block : (n + 1) * block] = jnp.where(
                    ids == wanted, jnp.ones_like(ids), jnp.zeros_like(ids)
                )
        present = dot(own_hot[t], row_hot[t]) > 0.0
        rank = dot(ones_where(present), before)
        code = jnp.where(present, rank, -1.0)
        for c in range(pieces):
            wide[:, t * pieces + c, :] = code[:, c * LANES : (c + 1) * LANES]
        rank_ref[t] = rank.astype(BF16)
    code_ref[...] = wide[...].astype(BF16)


def weigh_kernel(rows_ref, lens_ref, w_ref, rank_ref, ct_ref, row_hot):
    tables, slots, samples = rows_ref.shape
    owners, own_rows = rank_ref.shape[1:]
    shift = own_rows.bit_length() - 1
    owner_ids = iota((owners, samples), 0)
    chunk = 256
    chunk_ids = iota((chunk, samples), 0)
    for t in range(tables):
        rows = rows_ref[t]
        own = rows >> shift
        loc = (rows & (own_rows - 1)).astype(F32)
        usable = iota((slots, samples), 0) < lens_ref[t : t + 1, :]
        mass = jnp.where(usable, w_ref[t].astype(F32), 0.0)
        for l in range(slots):
            fill_row_hot(row_hot, l, loc[l : l + 1, :])
        look = dot(rank_ref[t], row_hot[...])
        spots = []
        for l in range(slots):
            cols = slice(l * samples, (l + 1) * samples)
            found = jnp.where(owner_ids == own[l : l + 1, :], look[:, cols], 0.0)
            rank_l = jnp.sum(found, axis=0, keepdims=True).astype(jnp.int32)
            spots.append(own[l : l + 1, :] * CAP + rank_l)

        def fill(step, _, t=t, spots=spots, mass=mass):
            base = pl.multiple_of(step * chunk, chunk)
            acc = jnp.zeros((chunk, samples), F32)
            for l in range(slots):
                acc = acc + jnp.where(chunk_ids == spots[l] - base, mass[l : l + 1, :], 0.0)
            ct_ref[t, pl.ds(base, chunk), :] = acc.astype(BF16)
            return 0

        lax.fori_loop(0, owners * CAP // chunk, fill, 0)


def hot_rows(codes, rank_ids, t, pieces):
    return [
        matches(rank_ids, codes[t * pieces + c : t * pieces + c + 1, :])
        for c in range(pieces)
    ]


def low_kernel(tables, emb_ref, low_ref):
    own_rows, width = low_ref.shape[1:]
    halves = width // LANES
    for t in range(tables):
        for h in range(halves):
            view = pl.ds(h * tables + t, own_rows, stride=tables * halves)
            low_ref[t, :, h * LANES : (h + 1) * LANES] = emb_ref[view, :].astype(BF16)


def fetch_kernel(code_ref, low_ref, out_hbm, hot, out, sems):
    devices = code_ref.shape[0]
    tables = low_ref.shape[0]
    pieces = code_ref.shape[1] // tables
    group = hot.shape[2] // CAP
    steps = devices // group
    rank_ids = iota((CAP, LANES), 0).astype(F32).astype(BF16)

    def send(step):
        block = pl.ds(step * group, group)
        return pltpu.make_async_copy(out.at[block], out_hbm.at[block], sems.at[step])

    for step in range(steps):
        first = step * group
        slot = hot.at[step % 2]
        for d in range(group):
            codes = code_ref[first + d].astype(F32)
            for t in range(tables):
                for c, part in enumerate(hot_rows(codes, rank_ids, t, pieces)):
                    slot[t, d * CAP : (d + 1) * CAP, c * LANES : (c + 1) * LANES] = part
        for t in range(tables):
            got = dot(slot[t], low_ref[t]).astype(BF16)
            out[first : first + group, t * CAP : (t + 1) * CAP, :] = got.reshape(group, CAP, -1)
        send(step).start()
    for step in range(steps):
        send(step).wait()


def dense_kernel(
    ct_ref, dense_ref, labels_ref, head_ref, got_hbm, cross_hbm, hidden_hbm, out_hbm,
    got, cross, hidden_w, joined, before, out_grad, out, sems, out_sems,
):
    tables, spots, samples = ct_ref.shape
    owners = spots // CAP
    width = dense_ref.shape[1]
    units = hidden_w.shape[1]
    chunk = 1024
    take_got = [
        pltpu.make_async_copy(got_hbm.at[:, pl.ds(t * CAP, CAP), :], got.at[t], sems.at[t])
        for t in range(tables)
    ]
    take_cross = pltpu.make_async_copy(cross_hbm, cross, sems.at[tables])
    take_hidden = [
        pltpu.make_async_copy(
            hidden_hbm.at[:, pl.ds(n * chunk, chunk)],
            hidden_w.at[:, pl.ds(n * chunk, chunk)],
            sems.at[tables + 1 + n],
        )
        for n in range(units // chunk)
    ]
    for copy in take_got + [take_cross] + take_hidden:
        copy.start()
    joined[:, :width] = dense_ref[...]
    for t in range(tables):
        take_got[t].wait()
        rows = got[t].reshape(spots, width)
        joined[:, (t + 1) * width : (t + 2) * width] = dot(ct_ref[t], rows, TN).astype(BF16)
    take_cross.wait()
    widened = joined[...].astype(F32)
    crossed = dot(joined[...], cross[...])
    layered = (widened * crossed + widened).astype(BF16)
    logits = jnp.zeros((samples, LANES), F32)
    for n in range(units // chunk):
        cols = slice(n * chunk, (n + 1) * chunk)
        take_hidden[n].wait()
        part = dot(layered, hidden_w[:, cols])
        before[:, cols] = part
        active = jnp.maximum(part, 0.0).astype(BF16).astype(F32)
        active = active * head_ref[:, cols]
        for m in range(chunk // LANES):
            logits = logits + active[:, m * LANES : (m + 1) * LANES]
    logits = jnp.sum(logits, axis=1, keepdims=True)
    diagonal = iota((samples, samples), 0) == iota((samples, samples), 1)
    marks = jnp.sum(
        jnp.where(diagonal, labels_ref[...].astype(F32), 0.0), axis=1, keepdims=True
    )
    slope = (jax.nn.sigmoid(logits) - marks) * loss_scale
    back = jnp.zeros((samples, layered.shape[1]), F32)
    for n in range(units // chunk):
        cols = slice(n * chunk, (n + 1) * chunk)
        out_grad[:, cols] = jnp.where(
            before[:, cols] > 0.0, slope * head_ref[:, cols], 0.0
        ).astype(BF16)
    back = dot(out_grad[...], hidden_w[...], NT)
    mixed = (back * widened).astype(BF16)
    steps = out_sems.shape[1]
    part_rows = spots // steps
    part_owners = owners // steps

    def send(t, n):
        block = (pl.ds(n * part_owners, part_owners), pl.ds(t * CAP, CAP))
        return pltpu.make_async_copy(out.at[block], out_hbm.at[block], out_sems.at[t, n])

    for t in range(tables):
        cols = slice((t + 1) * width, (t + 2) * width)
        total = back[:, cols] * (crossed[:, cols] + 1.0) + dot(mixed, cross[cols, :], NT)
        grads = total.astype(BF16)
        for n in range(steps):
            share = dot(ct_ref[t, n * part_rows : (n + 1) * part_rows, :], grads).astype(BF16)
            block = slice(n * part_owners, (n + 1) * part_owners)
            out[block, t * CAP : (t + 1) * CAP, :] = share.reshape(part_owners, CAP, width)
            send(t, n).start()
    for t in range(tables):
        for n in range(steps):
            send(t, n).wait()


def spread_kernel(tables, code_ref, second_ref, *refs):
    hot_refs, (columns_ref, tall) = refs[:tables], refs[tables:]
    devices = code_ref.shape[0]
    pieces = code_ref.shape[1] // tables
    count = tables * pieces
    rank_ids = iota((CAP, LANES), 0).astype(F32).astype(BF16)
    group = LANES // CAP

    def body(step, top):
        first = step * group
        codes = [code_ref[first + d].astype(F32) for d in range(group)]
        for t in range(tables):
            parts = [hot_rows(code, rank_ids, t, pieces) for code in codes]
            for c in range(pieces):
                block = jnp.concatenate([part[c] for part in parts], axis=0)
                hot_refs[t][
                    c * LANES : (c + 1) * LANES, pl.ds(pl.multiple_of(step * LANES, LANES), LANES)
                ] = jnp.transpose(block).astype(HOT)
        for code in codes:
            top = jnp.maximum(top, code)
        return top

    top = lax.fori_loop(0, devices // group, body, jnp.full((count, LANES), -1.0, F32))
    tall[...] = jnp.zeros_like(tall)
    tall[:count, :] = top
    for t in range(tables):
        for c in range(pieces):
            at = count + t * pieces + c
            tall[at : at + 1, :] = second_ref[t : t + 1, c * LANES : (c + 1) * LANES]
    columns_ref[...] = jnp.transpose(tall[...])


def collect_kernel(t, tables, hot_ref, columns_ref, share_ref, out_ref):
    own_rows, spots = hot_ref.shape
    width = share_ref.shape[2]
    pieces = own_rows // LANES
    lane_ids = iota((LANES, LANES), 1)
    stats = jnp.zeros((LANES, LANES), F32)
    shares = share_ref[:, t * CAP : (t + 1) * CAP, :].reshape(spots, width)
    for c in range(pieces):
        at = t * pieces + c
        grad = dot(hot_ref[c * LANES : (c + 1) * LANES, :].astype(BF16), shares)
        touched = columns_ref[:, at : at + 1] >= 0.0
        at = at + tables * pieces
        second = columns_ref[:, at : at + 1]
        mean = jnp.mean(grad * grad, axis=1, keepdims=True)
        second = jnp.where(touched, beta_second * second + (1.0 - beta_second) * mean, second)
        scale = jnp.where(touched, 1.0 / (jnp.sqrt(second) + epsilon), 0.0)
        decay = jnp.where(touched, beta_first, 1.0)
        stats = jnp.where(lane_ids == c, second, stats)
        stats = jnp.where(lane_ids == pieces + c, scale, stats)
        stats = jnp.where(lane_ids == 2 * pieces + c, decay, stats)
        out_ref[c * LANES : (c + 1) * LANES, :] = (1.0 - beta_first) * grad
    half = LANES // 2
    out_ref[own_rows:, :LANES] = stats[:half, :]
    out_ref[own_rows:, LANES:] = stats[half:, :]


def adam_kernel(tables, *refs):
    mine_refs, peer_refs = refs[:tables], refs[tables : 2 * tables]
    first_ref, first_out, second_out, step_out = refs[2 * tables :]
    own_rows = second_out.shape[1]
    width = mine_refs[0].shape[1]
    pieces = own_rows // LANES
    halves = width // LANES
    for t in range(tables):
        pair = (mine_refs[t], peer_refs[t])
        stats = [
            jnp.concatenate([ref[own_rows:, :LANES], ref[own_rows:, LANES:]], axis=0)
            for ref in pair
        ]
        second = jnp.transpose((stats[0] + stats[1]) * 0.5)
        for c in range(pieces):
            rows = slice(c * LANES, (c + 1) * LANES)
            second_out[t : t + 1, rows] = second[c : c + 1, :]
            scales = [
                jnp.broadcast_to(s[:, pieces + c : pieces + c + 1] * 0.5, (LANES, LANES))
                for s in stats
            ]
            decays = [
                jnp.broadcast_to(s[:, 2 * pieces + c : 2 * pieces + c + 1], (LANES, LANES))
                for s in stats
            ]
            for h in range(halves):
                view = pl.ds(
                    c * LANES * tables * halves + h * tables + t, LANES, stride=tables * halves
                )
                first = first_ref[view, :]
                cols = slice(h * LANES, (h + 1) * LANES)
                firsts = [decay * first + ref[rows, cols] for decay, ref in zip(decays, pair)]
                first_out[view, :] = (firsts[0] + firsts[1]) * 0.5
                step_out[view, :] = firsts[0] * scales[0] + firsts[1] * scales[1]


def to_rows(x):
    rows, tables, width = x.shape
    split = x.reshape(rows, tables, width // LANES, LANES)
    return jnp.transpose(split, (0, 2, 1, 3)).reshape(-1, LANES)


def from_rows(x, rows, tables, width):
    split = x.reshape(rows, width // LANES, tables, LANES)
    return jnp.transpose(split, (0, 2, 1, 3)).reshape(rows, tables, width)


def call(body, mib, out_shape, scratch, *operands, in_hbm=(), out_hbm=False):
    vmem = pl.BlockSpec(memory_space=pltpu.VMEM)
    hbm = pl.BlockSpec(memory_space=pltpu.HBM)
    single = not isinstance(out_shape, tuple)
    return pl.pallas_call(
        body,
        out_shape=out_shape,
        in_specs=[hbm if n in in_hbm else vmem for n in range(len(operands))],
        out_specs=(hbm if out_hbm else vmem) if single else tuple(vmem for _ in out_shape),
        scratch_shapes=scratch,
        compiler_params=pltpu.CompilerParams(vmem_limit_bytes=mib * MIB),
    )(*operands)


def local(
    owners,
    dense_input,
    bag_rows,
    bag_lengths,
    bag_weights,
    labels,
    embedding,
    first_moment,
    second_moment,
    cross_weight,
    hidden_weight,
    head_weight,
):
    samples, tables, slots = bag_rows.shape
    own_rows, _, width = embedding.shape
    pieces = own_rows // LANES
    count = tables * pieces
    spots = owners * CAP
    shape = jax.ShapeDtypeStruct
    rows = jnp.transpose(bag_rows, (1, 2, 0))
    lens = jnp.transpose(bag_lengths)
    code, rank = call(
        functools.partial(index_kernel, owners, own_rows),
        56,
        (
            shape((owners, count, LANES), BF16),
            shape((tables, owners, own_rows), BF16),
        ),
        [
            pltpu.VMEM((tables, owners, slots * samples), BF16),
            pltpu.VMEM((tables, slots * samples, own_rows), BF16),
            pltpu.VMEM((owners, count, LANES), F32),
        ],
        rows,
        lens,
    )
    asked = lax.all_to_all(code, "shard", 0, 0, tiled=True)
    low = call(
        functools.partial(low_kernel, tables),
        6,
        shape((tables, own_rows, width), BF16),
        [],
        to_rows(embedding),
    )
    found = call(
        fetch_kernel,
        50,
        shape((owners, tables * CAP, width), BF16),
        [
            pltpu.VMEM((2, tables, GROUP * CAP, own_rows), BF16),
            pltpu.VMEM((owners, tables * CAP, width), BF16),
            pltpu.SemaphoreType.DMA((owners // GROUP,)),
        ],
        asked,
        low,
        out_hbm=True,
    )
    got = lax.all_to_all(found, "shard", 0, 0, tiled=True)
    ct = call(
        weigh_kernel,
        12,
        shape((tables, spots, samples), BF16),
        [pltpu.VMEM((own_rows, slots * samples), BF16)],
        rows,
        lens,
        jnp.transpose(bag_weights, (1, 2, 0)),
        rank,
    )
    share = call(
        dense_kernel,
        50,
        shape((owners, tables * CAP, width), BF16),
        [
            pltpu.VMEM((tables, owners, CAP, width), BF16),
            pltpu.VMEM(cross_weight.shape, BF16),
            pltpu.VMEM(hidden_weight.shape, BF16),
            pltpu.VMEM((samples, cross_weight.shape[0]), BF16),
            pltpu.VMEM((samples, hidden_weight.shape[1]), F32),
            pltpu.VMEM((samples, hidden_weight.shape[1]), BF16),
            pltpu.VMEM((owners, tables * CAP, width), BF16),
            pltpu.SemaphoreType.DMA((tables + 1 + hidden_weight.shape[1] // 1024,)),
            pltpu.SemaphoreType.DMA((tables, 4)),
        ],
        ct,
        dense_input,
        labels.reshape(1, samples),
        head_weight.astype(F32).reshape(1, -1),
        got,
        cross_weight,
        hidden_weight,
        in_hbm=(4, 5, 6),
        out_hbm=True,
    )
    shares = lax.all_to_all(share, "shard", 0, 0, tiled=True)
    asked_later, _ = lax.optimization_barrier((asked, share))
    *hots, columns = call(
        functools.partial(spread_kernel, tables),
        52,
        tuple(shape((own_rows, spots), HOT) for _ in range(tables))
        + (shape((LANES, LANES), F32),),
        [pltpu.VMEM((LANES, LANES), F32)],
        asked_later,
        jnp.transpose(second_moment),
    )
    mine, peer = [], []
    for t in range(tables):
        part = call(
            functools.partial(collect_kernel, t, tables),
            14,
            shape((own_rows + LANES // 2, width), F32),
            [],
            hots[t],
            columns,
            shares,
        )
        mine.append(part)
        peer.append(lax.ppermute(part, "replica", [(0, 1), (1, 0)]))
    first, second, step = call(
        functools.partial(adam_kernel, tables),
        12,
        (
            shape((own_rows * tables * width // LANES, LANES), F32),
            shape((tables, own_rows), F32),
            shape((own_rows * tables * width // LANES, LANES), F32),
        ),
        [],
        *mine,
        *peer,
        to_rows(first_moment),
    )
    return (
        from_rows(first, own_rows, tables, width),
        jnp.transpose(second),
        from_rows(step, own_rows, tables, width),
    )


def solution(mesh):
    placed = (
        P(("replica", "shard"), None),
        P(("replica", "shard"), None, None),
        P(("replica", "shard"), None),
        P(("replica", "shard"), None, None),
        P(("replica", "shard")),
        P("shard", None, None),
        P("shard", None, None),
        P("shard", None),
        P(),
        P(),
        P(),
    )
    return jax.shard_map(
        functools.partial(local, mesh.shape["shard"]),
        mesh=mesh,
        in_specs=placed,
        out_specs=(P("shard", None, None), P("shard", None), P("shard", None, None)),
        check_vma=False,
    )
```

```python
import functools

import jax
import jax.numpy as jnp
from jax import lax
from jax.experimental import pallas as pl
from jax.experimental.pallas import tpu as pltpu
from jax.sharding import PartitionSpec as P

loss_scale = 64.0
beta_first = 0.9
beta_second = 0.99
epsilon = 1e-08

CAP = 32
LANES = 128
GROUP = 32
F32 = jnp.float32
BF16 = jnp.bfloat16
HOT = jnp.float8_e4m3fn
MIB = 1024 * 1024

NN = (((1,), (0,)), ((), ()))
NT = (((1,), (1,)), ((), ()))
TN = (((0,), (0,)), ((), ()))


def dot(a, b, dims=NN):
    return lax.dot_general(a, b, dims, preferred_element_type=F32)


def iota(shape, axis, dtype=jnp.int32):
    return lax.broadcasted_iota(dtype, shape, axis)


def ones_where(mask):
    return jnp.where(mask, 1.0, 0.0).astype(BF16)


def matches(ids, row):
    wanted = jnp.broadcast_to(row, ids.shape).astype(BF16)
    return jnp.where(ids == wanted, jnp.ones_like(ids), jnp.zeros_like(ids))


def fill_row_hot(row_hot, l, row):
    own_rows = row_hot.shape[0]
    samples = row.shape[1]
    block = 256
    ids = iota((block, samples), 0).astype(F32).astype(BF16)
    for n in range(own_rows // block):
        inside = row - n * block
        inside = jnp.where((inside >= 0.0) & (inside < block), inside, -1.0)
        row_hot[n * block : (n + 1) * block, l * samples : (l + 1) * samples] = matches(ids, inside)


def index_kernel(owners, own_rows, rows_ref, lens_ref, code_ref, rank_ref, own_hot, row_hot, wide):
    tables, slots, samples = rows_ref.shape
    shift = own_rows.bit_length() - 1
    pieces = own_rows // LANES
    before = ones_where(iota((own_rows, own_rows), 0) < iota((own_rows, own_rows), 1))
    owner_ids = iota((owners, samples), 0).astype(F32).astype(BF16)
    block = 256
    ids = iota((samples, block), 1).astype(F32).astype(BF16)
    for t in range(tables):
        rows = rows_ref[t]
        usable = iota((slots, samples), 0) < lens_ref[t : t + 1, :]
        own = jnp.where(usable, rows >> shift, -1).astype(F32)
        loc = (rows & (own_rows - 1)).astype(F32)
        columns = []
        for n in range(own_rows // block):
            inside = loc - n * block
            inside = jnp.where((inside >= 0.0) & (inside < block), inside, -1.0)
            columns.append(jnp.transpose(inside))
        for l in range(slots):
            cols = slice(l * samples, (l + 1) * samples)
            own_hot[t, :, cols] = matches(owner_ids, own[l : l + 1, :])
            for n, column in enumerate(columns):
                wanted = jnp.broadcast_to(column[:, l : l + 1], ids.shape).astype(BF16)
                row_hot[t, cols, n * block : (n + 1) * block] = jnp.where(
                    ids == wanted, jnp.ones_like(ids), jnp.zeros_like(ids)
                )
        present = dot(own_hot[t], row_hot[t]) > 0.0
        rank = dot(ones_where(present), before)
        code = jnp.where(present, rank, -1.0)
        for c in range(pieces):
            wide[:, t * pieces + c, :] = code[:, c * LANES : (c + 1) * LANES]
        rank_ref[t] = rank.astype(BF16)
    code_ref[...] = wide[...].astype(BF16)


def weigh_kernel(rows_ref, lens_ref, w_ref, rank_ref, ct_ref, row_hot):
    tables, slots, samples = rows_ref.shape
    owners, own_rows = rank_ref.shape[1:]
    shift = own_rows.bit_length() - 1
    owner_ids = iota((owners, samples), 0)
    chunk = 256
    chunk_ids = iota((chunk, samples), 0)
    for t in range(tables):
        rows = rows_ref[t]
        own = rows >> shift
        loc = (rows & (own_rows - 1)).astype(F32)
        usable = iota((slots, samples), 0) < lens_ref[t : t + 1, :]
        mass = jnp.where(usable, w_ref[t].astype(F32), 0.0)
        for l in range(slots):
            fill_row_hot(row_hot, l, loc[l : l + 1, :])
        look = dot(rank_ref[t], row_hot[...])
        spots = []
        for l in range(slots):
            cols = slice(l * samples, (l + 1) * samples)
            found = jnp.where(owner_ids == own[l : l + 1, :], look[:, cols], 0.0)
            rank_l = jnp.sum(found, axis=0, keepdims=True).astype(jnp.int32)
            spots.append(own[l : l + 1, :] * CAP + rank_l)

        def fill(step, _, t=t, spots=spots, mass=mass):
            base = pl.multiple_of(step * chunk, chunk)
            acc = jnp.zeros((chunk, samples), F32)
            for l in range(slots):
                acc = acc + jnp.where(chunk_ids == spots[l] - base, mass[l : l + 1, :], 0.0)
            ct_ref[t, pl.ds(base, chunk), :] = acc.astype(BF16)
            return 0

        lax.fori_loop(0, owners * CAP // chunk, fill, 0)


def hot_rows(codes, rank_ids, t, pieces):
    return [
        matches(rank_ids, codes[t * pieces + c : t * pieces + c + 1, :])
        for c in range(pieces)
    ]


def low_kernel(tables, emb_ref, low_ref):
    own_rows, width = low_ref.shape[1:]
    halves = width // LANES
    for t in range(tables):
        for h in range(halves):
            view = pl.ds(h * tables + t, own_rows, stride=tables * halves)
            low_ref[t, :, h * LANES : (h + 1) * LANES] = emb_ref[view, :].astype(BF16)


def fetch_kernel(code_ref, low_ref, out_hbm, hot, out, sems):
    devices = code_ref.shape[0]
    tables = low_ref.shape[0]
    pieces = code_ref.shape[1] // tables
    group = hot.shape[2] // CAP
    steps = devices // group
    rank_ids = iota((CAP, LANES), 0).astype(F32).astype(BF16)

    def send(step):
        block = pl.ds(step * group, group)
        return pltpu.make_async_copy(out.at[block], out_hbm.at[block], sems.at[step])

    for step in range(steps):
        first = step * group
        slot = hot.at[step % 2]
        for d in range(group):
            codes = code_ref[first + d].astype(F32)
            for t in range(tables):
                for c, part in enumerate(hot_rows(codes, rank_ids, t, pieces)):
                    slot[t, d * CAP : (d + 1) * CAP, c * LANES : (c + 1) * LANES] = part
        for t in range(tables):
            got = dot(slot[t], low_ref[t]).astype(BF16)
            out[first : first + group, t * CAP : (t + 1) * CAP, :] = got.reshape(group, CAP, -1)
        send(step).start()
    for step in range(steps):
        send(step).wait()


def dense_kernel(
    ct_ref, dense_ref, labels_ref, head_ref, got_hbm, cross_hbm, hidden_hbm, out_hbm,
    got, cross, hidden_w, joined, before, out_grad, out, sems, out_sems,
):
    tables, spots, samples = ct_ref.shape
    owners = spots // CAP
    width = dense_ref.shape[1]
    units = hidden_w.shape[1]
    chunk = 1024
    take_got = [
        pltpu.make_async_copy(got_hbm.at[:, pl.ds(t * CAP, CAP), :], got.at[t], sems.at[t])
        for t in range(tables)
    ]
    take_cross = pltpu.make_async_copy(cross_hbm, cross, sems.at[tables])
    take_hidden = [
        pltpu.make_async_copy(
            hidden_hbm.at[:, pl.ds(n * chunk, chunk)],
            hidden_w.at[:, pl.ds(n * chunk, chunk)],
            sems.at[tables + 1 + n],
        )
        for n in range(units // chunk)
    ]
    for copy in take_got + [take_cross] + take_hidden:
        copy.start()
    joined[:, :width] = dense_ref[...]
    for t in range(tables):
        take_got[t].wait()
        rows = got[t].reshape(spots, width)
        joined[:, (t + 1) * width : (t + 2) * width] = dot(ct_ref[t], rows, TN).astype(BF16)
    take_cross.wait()
    widened = joined[...].astype(F32)
    crossed = dot(joined[...], cross[...])
    layered = (widened * crossed + widened).astype(BF16)
    logits = jnp.zeros((samples, LANES), F32)
    for n in range(units // chunk):
        cols = slice(n * chunk, (n + 1) * chunk)
        take_hidden[n].wait()
        part = dot(layered, hidden_w[:, cols])
        before[:, cols] = part
        active = jnp.maximum(part, 0.0).astype(BF16).astype(F32)
        active = active * head_ref[:, cols]
        for m in range(chunk // LANES):
            logits = logits + active[:, m * LANES : (m + 1) * LANES]
    logits = jnp.sum(logits, axis=1, keepdims=True)
    diagonal = iota((samples, samples), 0) == iota((samples, samples), 1)
    marks = jnp.sum(
        jnp.where(diagonal, labels_ref[...].astype(F32), 0.0), axis=1, keepdims=True
    )
    slope = (jax.nn.sigmoid(logits) - marks) * loss_scale
    back = jnp.zeros((samples, layered.shape[1]), F32)
    for n in range(units // chunk):
        cols = slice(n * chunk, (n + 1) * chunk)
        out_grad[:, cols] = jnp.where(
            before[:, cols] > 0.0, slope * head_ref[:, cols], 0.0
        ).astype(BF16)
    back = dot(out_grad[...], hidden_w[...], NT)
    mixed = (back * widened).astype(BF16)
    steps = out_sems.shape[1]
    part_rows = spots // steps
    part_owners = owners // steps

    def send(t, n):
        block = (pl.ds(n * part_owners, part_owners), pl.ds(t * CAP, CAP))
        return pltpu.make_async_copy(out.at[block], out_hbm.at[block], out_sems.at[t, n])

    for t in range(tables):
        cols = slice((t + 1) * width, (t + 2) * width)
        total = back[:, cols] * (crossed[:, cols] + 1.0) + dot(mixed, cross[cols, :], NT)
        grads = total.astype(BF16)
        for n in range(steps):
            share = dot(ct_ref[t, n * part_rows : (n + 1) * part_rows, :], grads).astype(BF16)
            block = slice(n * part_owners, (n + 1) * part_owners)
            out[block, t * CAP : (t + 1) * CAP, :] = share.reshape(part_owners, CAP, width)
            send(t, n).start()
    for t in range(tables):
        for n in range(steps):
            send(t, n).wait()


def spread_kernel(tables, code_ref, second_ref, *refs):
    hot_refs, (columns_ref, tall) = refs[:tables], refs[tables:]
    devices = code_ref.shape[0]
    pieces = code_ref.shape[1] // tables
    count = tables * pieces
    rank_ids = iota((CAP, LANES), 0).astype(F32).astype(BF16)
    group = LANES // CAP

    def body(step, top):
        first = step * group
        codes = [code_ref[first + d].astype(F32) for d in range(group)]
        for t in range(tables):
            parts = [hot_rows(code, rank_ids, t, pieces) for code in codes]
            for c in range(pieces):
                block = jnp.concatenate([part[c] for part in parts], axis=0)
                hot_refs[t][
                    c * LANES : (c + 1) * LANES, pl.ds(pl.multiple_of(step * LANES, LANES), LANES)
                ] = jnp.transpose(block).astype(HOT)
        for code in codes:
            top = jnp.maximum(top, code)
        return top

    top = lax.fori_loop(0, devices // group, body, jnp.full((count, LANES), -1.0, F32))
    tall[...] = jnp.zeros_like(tall)
    tall[:count, :] = top
    for t in range(tables):
        for c in range(pieces):
            at = count + t * pieces + c
            tall[at : at + 1, :] = second_ref[t : t + 1, c * LANES : (c + 1) * LANES]
    columns_ref[...] = jnp.transpose(tall[...])


def collect_kernel(t, tables, hot_ref, columns_ref, share_ref, out_ref):
    own_rows, spots = hot_ref.shape
    width = share_ref.shape[2]
    pieces = own_rows // LANES
    lane_ids = iota((LANES, LANES), 1)
    stats = jnp.zeros((LANES, LANES), F32)
    shares = share_ref[:, t * CAP : (t + 1) * CAP, :].reshape(spots, width)
    for c in range(pieces):
        at = t * pieces + c
        grad = dot(hot_ref[c * LANES : (c + 1) * LANES, :].astype(BF16), shares)
        touched = columns_ref[:, at : at + 1] >= 0.0
        at = at + tables * pieces
        second = columns_ref[:, at : at + 1]
        mean = jnp.mean(grad * grad, axis=1, keepdims=True)
        second = jnp.where(touched, beta_second * second + (1.0 - beta_second) * mean, second)
        scale = jnp.where(touched, 1.0 / (jnp.sqrt(second) + epsilon), 0.0)
        decay = jnp.where(touched, beta_first, 1.0)
        stats = jnp.where(lane_ids == c, second, stats)
        stats = jnp.where(lane_ids == pieces + c, scale, stats)
        stats = jnp.where(lane_ids == 2 * pieces + c, decay, stats)
        out_ref[c * LANES : (c + 1) * LANES, :] = (1.0 - beta_first) * grad
    out_ref[own_rows:, :LANES] = stats
    out_ref[own_rows:, LANES:] = jnp.zeros((LANES, width - LANES), F32)


def adam_kernel(tables, *refs):
    mine_refs, peer_refs = refs[:tables], refs[tables : 2 * tables]
    first_ref, first_out, second_out, step_out = refs[2 * tables :]
    own_rows = second_out.shape[1]
    width = mine_refs[0].shape[1]
    pieces = own_rows // LANES
    halves = width // LANES
    for t in range(tables):
        pair = (mine_refs[t], peer_refs[t])
        stats = [ref[own_rows:, :LANES] for ref in pair]
        second = jnp.transpose((stats[0] + stats[1]) * 0.5)
        for c in range(pieces):
            rows = slice(c * LANES, (c + 1) * LANES)
            second_out[t : t + 1, rows] = second[c : c + 1, :]
            scales = [
                jnp.broadcast_to(s[:, pieces + c : pieces + c + 1] * 0.5, (LANES, LANES))
                for s in stats
            ]
            decays = [
                jnp.broadcast_to(s[:, 2 * pieces + c : 2 * pieces + c + 1], (LANES, LANES))
                for s in stats
            ]
            for h in range(halves):
                view = pl.ds(
                    c * LANES * tables * halves + h * tables + t, LANES, stride=tables * halves
                )
                first = first_ref[view, :]
                cols = slice(h * LANES, (h + 1) * LANES)
                firsts = [decay * first + ref[rows, cols] for decay, ref in zip(decays, pair)]
                first_out[view, :] = (firsts[0] + firsts[1]) * 0.5
                step_out[view, :] = firsts[0] * scales[0] + firsts[1] * scales[1]


def to_rows(x):
    rows, tables, width = x.shape
    split = x.reshape(rows, tables, width // LANES, LANES)
    return jnp.transpose(split, (0, 2, 1, 3)).reshape(-1, LANES)


def from_rows(x, rows, tables, width):
    split = x.reshape(rows, width // LANES, tables, LANES)
    return jnp.transpose(split, (0, 2, 1, 3)).reshape(rows, tables, width)


def call(body, mib, out_shape, scratch, *operands, in_hbm=(), out_hbm=False):
    vmem = pl.BlockSpec(memory_space=pltpu.VMEM)
    hbm = pl.BlockSpec(memory_space=pltpu.HBM)
    single = not isinstance(out_shape, tuple)
    return pl.pallas_call(
        body,
        out_shape=out_shape,
        in_specs=[hbm if n in in_hbm else vmem for n in range(len(operands))],
        out_specs=(hbm if out_hbm else vmem) if single else tuple(vmem for _ in out_shape),
        scratch_shapes=scratch,
        compiler_params=pltpu.CompilerParams(vmem_limit_bytes=mib * MIB),
    )(*operands)


def local(
    owners,
    dense_input,
    bag_rows,
    bag_lengths,
    bag_weights,
    labels,
    embedding,
    first_moment,
    second_moment,
    cross_weight,
    hidden_weight,
    head_weight,
):
    samples, tables, slots = bag_rows.shape
    own_rows, _, width = embedding.shape
    pieces = own_rows // LANES
    count = tables * pieces
    spots = owners * CAP
    shape = jax.ShapeDtypeStruct
    rows = jnp.transpose(bag_rows, (1, 2, 0))
    lens = jnp.transpose(bag_lengths)
    code, rank = call(
        functools.partial(index_kernel, owners, own_rows),
        56,
        (
            shape((owners, count, LANES), BF16),
            shape((tables, owners, own_rows), BF16),
        ),
        [
            pltpu.VMEM((tables, owners, slots * samples), BF16),
            pltpu.VMEM((tables, slots * samples, own_rows), BF16),
            pltpu.VMEM((owners, count, LANES), F32),
        ],
        rows,
        lens,
    )
    asked = lax.all_to_all(code, "shard", 0, 0, tiled=True)
    low = call(
        functools.partial(low_kernel, tables),
        6,
        shape((tables, own_rows, width), BF16),
        [],
        to_rows(embedding),
    )
    found = call(
        fetch_kernel,
        50,
        shape((owners, tables * CAP, width), BF16),
        [
            pltpu.VMEM((2, tables, GROUP * CAP, own_rows), BF16),
            pltpu.VMEM((owners, tables * CAP, width), BF16),
            pltpu.SemaphoreType.DMA((owners // GROUP,)),
        ],
        asked,
        low,
        out_hbm=True,
    )
    got = lax.all_to_all(found, "shard", 0, 0, tiled=True)
    ct = call(
        weigh_kernel,
        12,
        shape((tables, spots, samples), BF16),
        [pltpu.VMEM((own_rows, slots * samples), BF16)],
        rows,
        lens,
        jnp.transpose(bag_weights, (1, 2, 0)),
        rank,
    )
    share = call(
        dense_kernel,
        50,
        shape((owners, tables * CAP, width), BF16),
        [
            pltpu.VMEM((tables, owners, CAP, width), BF16),
            pltpu.VMEM(cross_weight.shape, BF16),
            pltpu.VMEM(hidden_weight.shape, BF16),
            pltpu.VMEM((samples, cross_weight.shape[0]), BF16),
            pltpu.VMEM((samples, hidden_weight.shape[1]), F32),
            pltpu.VMEM((samples, hidden_weight.shape[1]), BF16),
            pltpu.VMEM((owners, tables * CAP, width), BF16),
            pltpu.SemaphoreType.DMA((tables + 1 + hidden_weight.shape[1] // 1024,)),
            pltpu.SemaphoreType.DMA((tables, 4)),
        ],
        ct,
        dense_input,
        labels.reshape(1, samples),
        head_weight.astype(F32).reshape(1, -1),
        got,
        cross_weight,
        hidden_weight,
        in_hbm=(4, 5, 6),
        out_hbm=True,
    )
    shares = lax.all_to_all(share, "shard", 0, 0, tiled=True)
    asked_later, _ = lax.optimization_barrier((asked, share))
    *hots, columns = call(
        functools.partial(spread_kernel, tables),
        52,
        tuple(shape((own_rows, spots), HOT) for _ in range(tables))
        + (shape((LANES, LANES), F32),),
        [pltpu.VMEM((LANES, LANES), F32)],
        asked_later,
        jnp.transpose(second_moment),
    )
    mine, peer = [], []
    for t in range(tables):
        part = call(
            functools.partial(collect_kernel, t, tables),
            14,
            shape((own_rows + LANES, width), F32),
            [],
            hots[t],
            columns,
            shares,
        )
        mine.append(part)
        peer.append(lax.ppermute(part, "replica", [(0, 1), (1, 0)]))
    first, second, step = call(
        functools.partial(adam_kernel, tables),
        12,
        (
            shape((own_rows * tables * width // LANES, LANES), F32),
            shape((tables, own_rows), F32),
            shape((own_rows * tables * width // LANES, LANES), F32),
        ),
        [],
        *mine,
        *peer,
        to_rows(first_moment),
    )
    return (
        from_rows(first, own_rows, tables, width),
        jnp.transpose(second),
        from_rows(step, own_rows, tables, width),
    )


def solution(mesh):
    placed = (
        P(("replica", "shard"), None),
        P(("replica", "shard"), None, None),
        P(("replica", "shard"), None),
        P(("replica", "shard"), None, None),
        P(("replica", "shard")),
        P("shard", None, None),
        P("shard", None, None),
        P("shard", None),
        P(),
        P(),
        P(),
    )
    return jax.shard_map(
        functools.partial(local, mesh.shape["shard"]),
        mesh=mesh,
        in_specs=placed,
        out_specs=(P("shard", None, None), P("shard", None), P("shard", None, None)),
        check_vma=False,
    )
```
